256 devices in a mesh: dof: 128 (over z_hi, x, y, core), mode: 2 (over z_lo).
Axes of the slice: x: 4, y: 4, z: 8 (z_hi: 4, z_lo: 2; z = z_hi * 2 + z_lo), core: 2. Of those that a mesh axis runs over, the one named last changes fastest.
Arguments:
- stiffness_tiles: bfloat16 [4096, 10, 128, 128], P('dof'), may hold values from -0.15625 to 0.15625
- tile_cols: int32 [4096, 10], P('dof'), may hold values from 0 to 47, as said below
- send_rows: int32 [256, 8], P('dof'), may hold values from 0 to 31, as said below
- block: bfloat16 [524288, 128], P('dof', 'mode'), may hold values from -51 to 51
- lower_bound: float32 [1], replicated, may hold values from -1.2 to -0.6
- upper_bound: float32 [1], replicated, may hold values from 0.4 to 0.9
Outputs:
- basis: bfloat16 [524288, 128], P('dof', 'mode')
- ritz: float32 [128, 128], replicated
The draws below stay inside these ranges and needn't reach their ends.
Inputs may be any that keep to these rules, and one draw needn't show every extreme that they name: `tile_cols`: entry 0 of every tile row is that row's own local index; entry 1 is a code of the lower neighbour's upward list and entry 2 a code of the upper neighbour's downward list. A code below 32 is a tile row of the same partition; 32 + s is slot s of the lower neighbour's upward list; 40 + s is slot s of the upper neighbour's downward list. `send_rows`: rows 2 p and 2 p + 1 hold distinct local tile rows of partition p: its downward and upward send lists.
All inputs are finite; a program needn't handle non-finite values.
Results may differ from the reference program's by a relative error of at most 0.0086.
Values may be sent and summed in bfloat16 or wider, within the bound.
No kernel may reach another device: no remote copies, remote signals or barrier semaphores. Data moves between devices by JAX's collectives and lax.ppermute only.
A program may use at most 64 MiB of HBM per device.

```python
import jax
import jax.numpy as jnp
from jax import lax

TILE = 128
MODES = 128
NNZ = 10
DEGREE = 2
ROWT = 32
NSEND = 8
TROWS = 4096
NDOF = 524288


def draw_block(key, part):
    key_base = jax.random.fold_in(key, 0)
    key_common = jax.random.fold_in(key, 2)
    key_weights = jax.random.fold_in(key, 3)
    shared_count = 8
    row_index = jnp.arange(NDOF, dtype=jnp.float32)[:, None]
    row_rise = 1.0 + 2.0 * row_index / NDOF
    mixing = jnp.clip(jax.random.normal(key_weights, (shared_count, MODES), jnp.float32), -4.0, 4.0)
    base_draw = jnp.clip(jax.random.normal(key_base, (NDOF, MODES), jnp.float32), -6.0, 6.0)
    common = jnp.clip(jax.random.normal(key_common, (NDOF, shared_count), jnp.float32), -4.0, 4.0)
    shared = 0.45 * jnp.dot(common, mixing, precision=lax.Precision.HIGHEST)
    values = (base_draw + shared) * row_rise
    return jnp.clip(values, -51.0, 51.0).astype(jnp.bfloat16)


def draw_tile_cols(key, part):
    key_pick, key_local, key_ghost, key_low, key_up = jax.random.split(key, 5)
    local_col = jax.random.randint(key_local, (TROWS, NNZ), 0, ROWT)
    ghost_col = jax.random.randint(key_ghost, (TROWS, NNZ), ROWT, ROWT + 2 * NSEND)
    chooser = jax.random.randint(key_pick, (TROWS, NNZ), 0, 10)
    picked = jnp.where(chooser < 3, ghost_col, local_col)
    low_col = jax.random.randint(key_low, (TROWS, NNZ), ROWT, ROWT + NSEND)
    up_col = jax.random.randint(key_up, (TROWS, NNZ), ROWT + NSEND, ROWT + 2 * NSEND)
    own_row = (jnp.arange(TROWS, dtype=jnp.int32) % ROWT)[:, None]
    column = jnp.arange(NNZ, dtype=jnp.int32)[None, :]
    picked = jnp.where(column == 1, low_col, jnp.where(column == 2, up_col, picked))
    return jnp.where(column == 0, own_row, picked).astype(jnp.int32)


def draw_send_rows(key, part):
    list_count = 2 * (TROWS // ROWT)
    scores = jax.random.randint(key, (list_count, ROWT), 0, 1 << 20) * ROWT + jnp.arange(ROWT, dtype=jnp.int32)[None, :]
    ordering = jnp.argsort(scores, axis=-1, stable=True)
    return ordering[:, :NSEND].astype(jnp.int32)


def shard_levels(key, shape, cuts, least, high):
    level, own = 1.0, jax.random.fold_in(key, 6)
    for dim, shards_of in cuts:
        heights = jnp.exp(jax.random.uniform(jax.random.fold_in(own, dim), (shards_of,), jnp.float32, least / len(cuts), high / len(cuts)))
        level = level * jnp.repeat(heights, shape[dim] // shards_of).reshape([-1 if axis == dim else 1 for axis in range(len(shape))])
    return level


def noise(rng, dims, width, reach, cuts=(), held_as=jnp.bfloat16):
    loudness = shard_levels(rng, dims, cuts, -0.22, 0.18) if cuts else 1.0
    values = jax.random.normal(rng, dims, jnp.float32) * width * loudness
    return jnp.minimum(jnp.maximum(values, -reach), reach).astype(held_as)


def setup_inputs(seed: int = 0) -> dict:
    splits = jax.random.split(jax.random.key(seed), 7)
    return {
        "stiffness_tiles": noise(splits[0], (TROWS, NNZ, TILE, TILE), (NNZ * TILE) ** -0.5, 0.15625, ((0, 128),)),
        "tile_cols": draw_tile_cols(jax.random.fold_in(splits[6], 71), 0),
        "send_rows": draw_send_rows(jax.random.fold_in(splits[6], 71), 0),
        "block": draw_block(jax.random.fold_in(splits[6], 71), 0),
        "lower_bound": jnp.clip(jax.random.uniform(splits[4], (1,), jnp.float32, -1.2, -0.6), -1.2, -0.6),
        "upper_bound": jnp.clip(jax.random.uniform(splits[5], (1,), jnp.float32, 0.4, 0.9), 0.4, 0.9),
    }


def apply_stiffness(stiffness_tiles, tile_cols, send_rows, field):
    part_count = TROWS // ROWT
    tile_view = field.reshape(TROWS, TILE, MODES)

    def partition_product(part_index):
        col_code = lax.dynamic_slice_in_dim(tile_cols, part_index * ROWT, ROWT, 0)
        lower_part = jnp.maximum(part_index - 1, 0).astype(jnp.int32)
        upper_part = jnp.minimum(part_index + 1, part_count - 1).astype(jnp.int32)
        low_rows = lax.dynamic_index_in_dim(send_rows, 2 * lower_part + 1, 0, keepdims=False)
        up_rows = lax.dynamic_index_in_dim(send_rows, 2 * upper_part, 0, keepdims=False)
        low_slot = jnp.clip(col_code - ROWT, 0, NSEND - 1)
        up_slot = jnp.clip(col_code - ROWT - NSEND, 0, NSEND - 1)
        source_row = jnp.where(col_code < ROWT, part_index * ROWT + col_code, jnp.where(col_code < ROWT + NSEND, lower_part * ROWT + low_rows[low_slot], upper_part * ROWT + up_rows[up_slot])).astype(jnp.int32)
        present = jnp.where(col_code < ROWT, True, jnp.where(col_code < ROWT + NSEND, part_index > 0, part_index < part_count - 1))
        blocks = tile_view[source_row].astype(jnp.float32) * present[:, :, None, None].astype(jnp.float32)
        row_tiles = lax.dynamic_slice_in_dim(stiffness_tiles, part_index * ROWT, ROWT, 0).astype(jnp.float32)
        return jnp.einsum('rkij,rkjm->rim', row_tiles, blocks)
    result = lax.map(partition_product, jnp.arange(part_count, dtype=jnp.int32))
    return result.reshape(NDOF, MODES)

def reference(stiffness_tiles, tile_cols, send_rows, block, lower_bound, upper_bound):
    center = (upper_bound[0] + lower_bound[0]) * 0.5
    half_width = (upper_bound[0] - lower_bound[0]) * 0.5
    previous = block
    current = ((apply_stiffness(stiffness_tiles, tile_cols, send_rows, block) - center * block.astype(jnp.float32)) / half_width).astype(jnp.bfloat16)
    for step in range(DEGREE - 1):
        following = (2.0 * (apply_stiffness(stiffness_tiles, tile_cols, send_rows, current) - center * current.astype(jnp.float32)) / half_width - previous.astype(jnp.float32)).astype(jnp.bfloat16)
        previous, current = (current, following)
    filtered = current
    image_block = apply_stiffness(stiffness_tiles, tile_cols, send_rows, filtered).astype(jnp.bfloat16)
    gram_matrix = jnp.dot(filtered.T.astype(jnp.float32), filtered.astype(jnp.float32), preferred_element_type=jnp.float32) / NDOF
    projected = jnp.dot(filtered.T.astype(jnp.float32), image_block.astype(jnp.float32), preferred_element_type=jnp.float32) / NDOF
    factor = jnp.linalg.cholesky(gram_matrix)
    identity = jnp.eye(MODES, dtype=jnp.float32)
    inverse = jax.scipy.linalg.solve_triangular(factor, identity, lower=True)
    ritz_matrix = jnp.dot(jnp.dot(inverse, projected, precision=lax.Precision.HIGHEST), inverse.T, precision=lax.Precision.HIGHEST)
    right_factor = inverse.T.astype(jnp.bfloat16)
    basis_out = jnp.dot(filtered.astype(jnp.float32), right_factor.astype(jnp.float32), preferred_element_type=jnp.float32).astype(jnp.bfloat16)
    return (basis_out, ritz_matrix)
```

```python
import functools

import jax
import jax.numpy as jnp
from jax import lax
from jax.experimental import pallas as pl
from jax.experimental.pallas import tpu as pltpu
from jax.sharding import Mesh
from jax.sharding import PartitionSpec as P

Z, X, Y, C, M = "dof_z", "dof_x", "dof_y", "dof_c", "mode"
DOF = (Z, X, Y, C)
VMEM = pl.BlockSpec(memory_space=pltpu.VMEM)
SMEM = pl.BlockSpec(memory_space=pltpu.SMEM)
NT = (((1,), (1,)), ((), ()))


def shifted(block, axis, distance):
    devices = range(lax.axis_size(axis))
    route = [(i - distance, i) for i in devices if i - distance in devices]
    return lax.ppermute(block, axis, route)


def flipped(block, axis, bits):
    return lax.ppermute(block, axis, [(i, i ^ bits) for i in range(lax.axis_size(axis))])


def copy_lists(send, field, up, down, tile):
    count = up.shape[1] // tile
    for slot in range(count):
        here = slice(slot * tile, (slot + 1) * tile)
        low = pl.multiple_of(send[slot] * tile, tile)
        high = pl.multiple_of(send[count + slot] * tile, tile)
        down[:, here] = field[:, pl.ds(low, tile)]
        up[:, here] = field[:, pl.ds(high, tile)]


def pick_lists(send_rows, field, tile):
    modes = field.shape[0]
    count = send_rows.shape[0] // 2
    part = jax.ShapeDtypeStruct((modes, count * tile), field.dtype)

    def kernel(send, field_ref, up, down):
        copy_lists(send, field_ref, up, down, tile)

    return pl.pallas_call(
        kernel,
        out_shape=(part, part),
        in_specs=[SMEM, VMEM],
        out_specs=(VMEM, VMEM),
        compiler_params=pltpu.CompilerParams(vmem_limit_bytes=8 << 20),
        name="pick_lists",
    )(send_rows, field)


def apply_operator(level, tiles, codes, send_rows, scales, field, previous, from_lower, from_upper):
    rows, nnz, tile, _ = tiles.shape
    modes, width = field.shape
    ghost = from_lower.shape[1]
    step_rows = 4
    lists = level < 3

    def kernel(*refs):
        codes, send, scales, tiles, field, *rest = refs
        if level == 2:
            previous, *rest = rest
        lower, upper, out, *rest = rest
        if lists:
            up, down, *rest = rest
        (extended,) = rest
        step = pl.program_id(0)

        @pl.when(step == 0)
        def _():
            extended[:, :width] = field[...]
            extended[:, width : width + ghost] = lower[...]
            extended[:, width + ghost :] = upper[...]

        center, factor = scales[0], scales[1]
        for sub in range(step_rows):
            row = step * step_rows + sub
            total = None
            for k in range(0, nnz, 2):
                sources = [
                    extended[:, pl.ds(pl.multiple_of(codes[row * nnz + k + i] * tile, tile), tile)]
                    for i in range(2)
                ]
                product = lax.dot_general(
                    jnp.concatenate(sources, axis=1),
                    jnp.concatenate([tiles[sub, k], tiles[sub, k + 1]], axis=1),
                    NT,
                    preferred_element_type=jnp.float32,
                )
                total = product if total is None else total + product
            here = pl.ds(pl.multiple_of(row * tile, tile), tile)
            if level < 3:
                total = (total - center * field[:, here].astype(jnp.float32)) * factor
            if level == 2:
                total = 2.0 * total - previous[:, here].astype(jnp.float32)
            out[:, here] = total.astype(out.dtype)

        if lists:

            @pl.when(step == pl.num_programs(0) - 1)
            def _():
                copy_lists(send, out, up, down, tile)

    operands = [codes, send_rows, scales, tiles, field]
    specs = [SMEM, SMEM, SMEM, pl.BlockSpec((step_rows, nnz, tile, tile), lambda i: (i, 0, 0, 0)), VMEM]
    if level == 2:
        operands.append(previous)
        specs.append(VMEM)
    operands += [from_lower, from_upper]
    specs += [VMEM, VMEM]
    shapes = [jax.ShapeDtypeStruct(field.shape, field.dtype)]
    if lists:
        shapes += [jax.ShapeDtypeStruct(from_lower.shape, field.dtype)] * 2
    return pl.pallas_call(
        kernel,
        grid=(rows // step_rows,),
        out_shape=shapes,
        in_specs=specs,
        out_specs=[VMEM] * len(shapes),
        scratch_shapes=[pltpu.VMEM((modes, width + 2 * ghost), field.dtype)],
        compiler_params=pltpu.CompilerParams(vmem_limit_bytes=16 << 20),
        cost_estimate=pl.CostEstimate(
            flops=2 * tiles.size * modes, bytes_accessed=tiles.size * 2, transcendentals=0
        ),
        name=f"apply_{level}",
    )(*operands)


def partial_sums(place, own, partner, image):
    modes, width = own.shape
    product = jax.ShapeDtypeStruct((modes, 2 * modes), jnp.float32)

    def kernel(place, own, partner, image, keep, send, both, left):
        mode, core = place[0], place[1]
        both[pl.ds(pl.multiple_of(mode * modes, modes), modes), :] = own[...]
        both[pl.ds(pl.multiple_of((1 - mode) * modes, modes), modes), :] = partner[...]
        left[pl.ds(pl.multiple_of(core * modes, modes), modes), :] = own[...]
        left[pl.ds(pl.multiple_of((1 - core) * modes, modes), modes), :] = image[...]
        sums = lax.dot_general(left[...], both[...], NT, preferred_element_type=jnp.float32)
        keep[...] = sums[:modes]
        send[...] = sums[modes:]

    return pl.pallas_call(
        kernel,
        out_shape=(product, product, jax.ShapeDtypeStruct((2 * modes, width), own.dtype)),
        in_specs=[SMEM, VMEM, VMEM, VMEM],
        out_specs=(VMEM, VMEM, VMEM),
        scratch_shapes=[pltpu.VMEM((2 * modes, width), own.dtype)],
        compiler_params=pltpu.CompilerParams(vmem_limit_bytes=16 << 20),
        name="partial_sums",
    )(place, own, partner, image)


def sum_over_chips(value):
    for axis in (X, Y, Z):
        others = [flipped(value, axis, bits) for bits in (1, 2, 3)]
        value = (value + others[0]) + (others[1] + others[2])
    return value


def reduce_factor(gram_matrix, projected):
    factor = jnp.linalg.cholesky(gram_matrix)
    identity = jnp.eye(gram_matrix.shape[0], dtype=jnp.float32)
    inverse = jax.scipy.linalg.solve_triangular(factor, identity, lower=True)
    ritz_matrix = jnp.dot(
        jnp.dot(inverse, projected, precision=lax.Precision.HIGHEST),
        inverse.T,
        precision=lax.Precision.HIGHEST,
    )
    return (ritz_matrix, inverse)


def shards(stiffness_tiles, tile_cols, send_rows, block, lower_bound, upper_bound):
    row_count, mode_cols = block.shape
    tile = stiffness_tiles.shape[2]
    dof_total = row_count * lax.axis_size(DOF)
    center = (upper_bound[0] + lower_bound[0]) * 0.5
    half_width = (upper_bound[0] - lower_bound[0]) * 0.5
    scales = jnp.stack([center, 1.0 / half_width])
    codes = tile_cols.reshape(-1)
    send = send_rows.reshape(-1)
    mode, core = lax.axis_index(M), lax.axis_index(C)
    place = jnp.stack([mode, core])

    def exchange(up, down):
        return shifted(up, DOF, 1), shifted(down, DOF, -1)

    apply = functools.partial(apply_operator, tiles=stiffness_tiles, codes=codes, send_rows=send, scales=scales)
    level_0 = block.T
    lower, upper = exchange(*pick_lists(send, level_0, tile))
    level_1, up, down = apply(1, field=level_0, previous=None, from_lower=lower, from_upper=upper)
    lower, upper = exchange(up, down)
    filtered, up, down = apply(2, field=level_1, previous=level_0, from_lower=lower, from_upper=upper)
    lower, upper = exchange(up, down)
    partner = flipped(filtered, M, 1)
    (image,) = apply(3, field=filtered, previous=None, from_lower=lower, from_upper=upper)
    keep, send_half, both = partial_sums(place, filtered, partner, image)
    half = sum_over_chips(keep + flipped(send_half, C, 1))
    others = [flipped(half, C, 1), flipped(half, M, 1), flipped(half, (C, M), 3)]
    same, swapped = (half, others[1]), (others[0], others[2])
    gram_rows = [jnp.where(core == 0, a, b) for a, b in zip(same, swapped)]
    proj_rows = [jnp.where(core == 0, b, a) for a, b in zip(same, swapped)]

    def in_order(rows):
        return jnp.where(mode == 0, jnp.concatenate(rows), jnp.concatenate(rows[::-1]))

    ritz_matrix, inverse = reduce_factor(in_order(gram_rows) / dof_total, in_order(proj_rows).T / dof_total)
    left = lax.dynamic_slice_in_dim(inverse, mode * mode_cols, mode_cols, 0).astype(jnp.bfloat16)
    basis = jnp.dot(left, both, preferred_element_type=jnp.float32).astype(jnp.bfloat16)
    return (basis.T, ritz_matrix)


def solution(mesh):
    torus = Mesh(mesh.devices.reshape(4, 4, 4, 2, mesh.shape["mode"]), DOF + (M,))
    return jax.shard_map(
        shards,
        mesh=torus,
        in_specs=(P(DOF, None, None, None), P(DOF, None), P(DOF, None), P(DOF, M), P(), P()),
        out_specs=(P(DOF, M), P()),
        check_vma=False,
    )
```

```python
import jax
import jax.numpy as jnp
from jax import lax
from jax.experimental import pallas as pl
from jax.experimental.pallas import tpu as pltpu
from jax.sharding import Mesh
from jax.sharding import PartitionSpec as P

Z, X, Y, C, M = "dof_z", "dof_x", "dof_y", "dof_c", "mode"
DOF = (Z, X, Y, C)
VMEM = pl.BlockSpec(memory_space=pltpu.VMEM)
SMEM = pl.BlockSpec(memory_space=pltpu.SMEM)
HBM = pl.BlockSpec(memory_space=pltpu.HBM)
NT = (((1,), (1,)), ((), ()))
GROUP = 8


def params(mib):
    return pltpu.CompilerParams(vmem_limit_bytes=mib << 20)


def shape(dims, dtype):
    return jax.ShapeDtypeStruct(dims, dtype)


def flipped(block, axis, bits):
    return lax.ppermute(block, axis, [(i, i ^ bits) for i in range(lax.axis_size(axis))])


def swapped_between_chips(block):
    count = lax.axis_size(DOF)
    pairs = [(i, i + 1) for i in range(1, count - 1, 2)]
    return lax.ppermute(block, DOF, pairs + [(b, a) for a, b in pairs])


def exchange(near, far):
    from_far = swapped_between_chips(far)
    from_near = flipped(near, C, 1)
    return from_near, from_far


def columns(index, tile):
    return pl.ds(pl.multiple_of(index * tile, tile), tile)


def copy_lists(place, send, field, near, far, tile):
    core = place[1]
    for slot in range(near.shape[1] // tile):
        here = slice(slot * tile, (slot + 1) * tile)
        near[:, here] = field[:, columns(send[1 - core, slot], tile)]
        far[:, here] = field[:, columns(send[core, slot], tile)]


def pick_lists(place, send_rows, field, tile):
    modes = field.shape[0]
    count = send_rows.shape[1]
    part = shape((modes, count * tile), field.dtype)

    def kernel(place, send, field, near, far, sems):
        core = place[1]
        copies = []
        for slot in range(count):
            here = slice(slot * tile, (slot + 1) * tile)
            for out, row, which in ((far, core, 0), (near, 1 - core, 1)):
                source = field.at[:, columns(send[row, slot], tile)]
                copies.append(pltpu.make_async_copy(source, out.at[:, here], sems.at[which, slot]))
        for copy in copies:
            copy.start()
        for copy in copies:
            copy.wait()

    return pl.pallas_call(
        kernel,
        out_shape=(part, part),
        in_specs=[SMEM, SMEM, HBM],
        out_specs=(VMEM, VMEM),
        scratch_shapes=[pltpu.SemaphoreType.DMA((2, count))],
        compiler_params=params(4),
        name="pick_lists",
    )(place, send_rows, pltpu.with_memory_space_constraint(field, pltpu.HBM))


class Plan:
    def __init__(self, rows, nnz):
        self.pairs = rows * ((nnz + 1) // 2) + GROUP
        self.tiles = 2 * self.pairs + 16
        self.rows = 2 * self.tiles
        self.groups = self.rows + self.pairs + 16
        self.size = self.groups + 8


def stage(tile_cols, tiles, ghosts):
    nnz, rows = tile_cols.shape
    plan = Plan(rows, nnz)
    chunks = 8
    per_chunk = rows * nnz // chunks

    def kernel(cols, tiles, staged, local, ghost, sems):
        copies = [
            pltpu.make_async_copy(
                tiles.at[pl.ds(i * per_chunk, per_chunk)], staged.at[pl.ds(i * per_chunk, per_chunk)], sems.at[i]
            )
            for i in range(chunks)
        ]
        for copy in copies:
            copy.start()

        lists = ((local, rows), (ghost, ghosts))

        def put(row, counts):
            starts = counts
            for k in range(nnz):
                code = cols[k, row]
                is_local = (code < rows).astype(jnp.int32)
                took = (is_local, 1 - is_local)
                for (out, _), at, shift in zip(lists, counts, (0, rows)):
                    out[at] = code - shift
                    out[plan.tiles + at] = row * nnz + k
                counts = tuple(at + one for at, one in zip(counts, took))
            for (out, zero), at, start in zip(lists, counts, starts):
                out[at] = jnp.int32(zero)
                out[plan.tiles + at] = row * nnz
                for i in range((nnz + 1) // 2):
                    out[plan.rows + (start >> 1) + i] = row
            return tuple(at + (at & 1) for at in counts)

        counts = lax.fori_loop(0, rows, put, (jnp.int32(0), jnp.int32(0)))
        for (out, zero), at in zip(lists, counts):
            for i in range(GROUP):
                for j in range(2):
                    out[at + 2 * i + j] = jnp.int32(zero)
                    out[plan.tiles + at + 2 * i + j] = jnp.int32(0)
                out[plan.rows + (at >> 1) + i] = jnp.int32(rows)
            out[plan.groups] = ((at >> 1) + GROUP - 1) // GROUP
        for copy in copies:
            copy.wait()

    return pl.pallas_call(
        kernel,
        out_shape=(shape(tiles.shape, tiles.dtype), shape((plan.size,), jnp.int32), shape((plan.size,), jnp.int32)),
        in_specs=[SMEM, HBM],
        out_specs=(VMEM, SMEM, SMEM),
        scratch_shapes=[pltpu.SemaphoreType.DMA((chunks,))],
        compiler_params=params(4),
        cost_estimate=pl.CostEstimate(flops=0, bytes_accessed=2 * tiles.size, transcendentals=0),
        name="stage",
    )(tile_cols, pltpu.with_memory_space_constraint(tiles, pltpu.HBM))


def add_pairs(layout, plan, tiles, sources, total):
    tile = tiles.shape[1]

    def step(group, carry):
        for u in range(GROUP):
            pair = group * GROUP + u
            source = [sources[:, columns(plan[2 * pair + i], tile)] for i in range(2)]
            stored = [tiles[plan[layout.tiles + 2 * pair + i]] for i in range(2)]
            product = lax.dot_general(
                jnp.concatenate(source, axis=1),
                jnp.concatenate(stored, axis=1),
                NT,
                preferred_element_type=jnp.float32,
            )
            here = columns(plan[layout.rows + pair], tile)
            total[:, here] = total[:, here] + product
        return carry

    lax.fori_loop(0, plan[layout.groups], step, 0)


def local_sums(level, layout, plan, tiles, field):
    modes, width = field.shape
    tile = tiles.shape[1]

    def kernel(plan, tiles, field, total, sources):
        sources[:, :width] = field[...]
        sources[:, width:] = jnp.zeros((modes, tile), field.dtype)
        total[...] = jnp.zeros(total.shape, total.dtype)
        add_pairs(layout, plan, tiles, sources, total)

    return pl.pallas_call(
        kernel,
        out_shape=shape((modes, width + tile), jnp.float32),
        in_specs=[SMEM, VMEM, VMEM],
        out_specs=VMEM,
        scratch_shapes=[pltpu.VMEM((modes, width + tile), field.dtype)],
        compiler_params=params(8),
        cost_estimate=pl.CostEstimate(flops=tiles.size * modes, bytes_accessed=2 * tiles.size, transcendentals=0),
        name=f"local_sums_{level}",
    )(plan, tiles, field)


def add_ghosts(layout, place, plan, tiles, near, far, ghosts, total):
    tile = tiles.shape[1]
    width = near.shape[1]
    core = place[1]
    ghosts[:, pl.ds(pl.multiple_of((1 - core) * width, width), width)] = near[...]
    ghosts[:, pl.ds(pl.multiple_of(core * width, width), width)] = far[...]
    ghosts[:, 2 * width :] = jnp.zeros((near.shape[0], tile), near.dtype)
    add_pairs(layout, plan, tiles, ghosts, total)


def next_level(level, layout, place, plan, send_rows, bounds, tiles, total, near, far, field, previous):
    modes, width = field.shape
    tile = tiles.shape[1]
    part = 4 * tile

    def kernel(place, plan, send, lower, upper, tiles, _, near, far, field, *rest):
        if level == 2:
            previous, *rest = rest
        total, out, near_out, far_out, ghosts = rest
        add_ghosts(layout, place, plan, tiles, near, far, ghosts, total)
        center = (upper[0] + lower[0]) * 0.5
        factor = 1.0 / jnp.full((modes, part), (upper[0] - lower[0]) * 0.5, jnp.float32)

        def finish(i, carry):
            here = columns(i, part)
            value = (total[:, here] - center * field[:, here].astype(jnp.float32)) * factor
            if level == 2:
                value = 2.0 * value - previous[:, here].astype(jnp.float32)
            out[:, here] = value.astype(out.dtype)
            return carry

        lax.fori_loop(0, width // part, finish, 0)
        copy_lists(place, send, out, near_out, far_out, tile)

    operands = [place, plan, send_rows, *bounds, tiles, total, near, far, field]
    specs = [SMEM] * 5 + [VMEM] * 5
    if level == 2:
        operands.append(previous)
        specs.append(VMEM)
    return pl.pallas_call(
        kernel,
        out_shape=(
            shape(total.shape, total.dtype),
            shape(field.shape, field.dtype),
            shape(near.shape, near.dtype),
            shape(near.shape, near.dtype),
        ),
        in_specs=specs,
        out_specs=(VMEM,) * 4,
        scratch_shapes=[pltpu.VMEM((modes, 2 * near.shape[1] + tile), near.dtype)],
        input_output_aliases={6: 0},
        compiler_params=params(8),
        name=f"next_level_{level}",
    )(*operands)[1:]


def partial_sums(layout, place, plan, tiles, total, near, far, own, partner):
    modes, width = own.shape
    tile = tiles.shape[1]
    product = shape((modes, 2 * modes), jnp.float32)

    def kernel(place, plan, tiles, _, near, far, own, partner, total, keep, send, both, ghosts, left):
        add_ghosts(layout, place, plan, tiles, near, far, ghosts, total)
        mode, core = place[0], place[1]
        both[columns(mode, modes), :] = own[...]
        both[columns(1 - mode, modes), :] = partner[...]
        left[columns(core, modes), :] = own[...]
        left[columns(1 - core, modes), :] = total[:, :width].astype(own.dtype)
        sums = lax.dot_general(left[...], both[...], NT, preferred_element_type=jnp.float32)
        keep[...] = sums[:modes]
        send[...] = sums[modes:]

    return pl.pallas_call(
        kernel,
        out_shape=(shape(total.shape, total.dtype), product, product, shape((2 * modes, width), own.dtype)),
        in_specs=[SMEM] * 2 + [VMEM] * 6,
        out_specs=(VMEM,) * 4,
        scratch_shapes=[
            pltpu.VMEM((modes, 2 * near.shape[1] + tile), near.dtype),
            pltpu.VMEM((2 * modes, width), own.dtype),
        ],
        input_output_aliases={3: 0},
        compiler_params=params(12),
        name="partial_sums",
    )(place, plan, tiles, total, near, far, own, partner)[1:]


def sum_over_chips(value):
    for axis in (X, Y, Z):
        others = [flipped(value, axis, bits) for bits in (1, 2, 3)]
        value = (value + others[0]) + (others[1] + others[2])
    return value


def spread(block, lane):
    return jnp.broadcast_to(block[:, lane : lane + 1], block.shape)


def eliminated(blocks):
    rows, size = blocks[0].shape
    sub = lax.broadcasted_iota(jnp.int32, (rows, size), 0)
    lane = lax.broadcasted_iota(jnp.int32, (rows, size), 1)
    blocks = list(blocks)
    for b in range(len(blocks)):
        first = rows * b
        row = [jnp.broadcast_to(blocks[b][s : s + 1, :], (rows, size)) for s in range(rows)]
        d = {(t, s): spread(row[t], first + s) for t in range(rows) for s in range(t + 1)}
        unit = [row[s] + (lane == first + s).astype(jnp.float32) for s in range(rows)]
        ratio, reciprocal = {}, []
        for s in range(rows):
            reciprocal.append(1.0 / d[s, s])
            for t in range(s + 1, rows):
                ratio[t, s] = d[t, s] * reciprocal[s]
            for t in range(s + 1, rows):
                for q in range(s + 1, t + 1):
                    d[t, q] = d[t, q] - ratio[t, s] * d[q, s]
                unit[t] = unit[t] - ratio[t, s] * unit[s]
        solved = [None] * rows
        for s in reversed(range(rows)):
            value = unit[s] * reciprocal[s]
            for t in range(s + 1, rows):
                value = value - ratio[t, s] * solved[t]
            solved[s] = value
        for k in range(b + 1, len(blocks)):
            value = blocks[k]
            for s in range(rows):
                value = value - spread(blocks[k], first + s) * solved[s]
            blocks[k] = value
        value = blocks[b]
        for s in range(rows):
            value = jnp.where(sub == s, unit[s] - (lane == first + s).astype(jnp.float32), value)
        blocks[b] = value
    return blocks


def factor_and_project(place, quarters, both, dof_total):
    modes, width = both.shape[0] // 2, both.shape[1]
    size = 2 * modes

    def kernel(place, own, other_core, other_mode, last, both, basis, ritz, sums, inverse):
        mode, core = place[0], place[1]
        for part, c, m in (
            (own, core, mode),
            (other_core, 1 - core, mode),
            (other_mode, core, 1 - mode),
            (last, 1 - core, 1 - mode),
        ):
            sums[columns(2 * c + m, modes), :] = part[...] / dof_total
        blocks = eliminated([sums[i : i + 8, :] for i in range(0, size, 8)])
        matrix = jnp.concatenate(blocks, axis=0)
        sub = lax.broadcasted_iota(jnp.int32, (size, size), 0)
        lane = lax.broadcasted_iota(jnp.int32, (size, size), 1)
        pivots = jnp.sum(jnp.where(sub == lane, matrix, 0.0), axis=1, keepdims=True)
        lower = jnp.where(lane < sub, matrix, jnp.where(lane == sub, 1.0, 0.0)) * lax.rsqrt(pivots)
        inverse[...] = lower
        left = inverse[columns(mode, modes), :].astype(both.dtype)
        basis[...] = jnp.dot(left, both[...], preferred_element_type=jnp.float32).astype(basis.dtype)
        half = lax.dot_general(
            lower, sums[size:, :], NT, precision=lax.Precision.HIGHEST, preferred_element_type=jnp.float32
        )
        ritz[...] = lax.dot_general(
            half, lower, NT, precision=lax.Precision.HIGHEST, preferred_element_type=jnp.float32
        )

    return pl.pallas_call(
        kernel,
        out_shape=(shape((modes, width), both.dtype), shape((size, size), jnp.float32)),
        in_specs=[SMEM] + [VMEM] * 5,
        out_specs=(VMEM, VMEM),
        scratch_shapes=[pltpu.VMEM((2 * size, size), jnp.float32), pltpu.VMEM((size, size), jnp.float32)],
        compiler_params=params(12),
        name="factor_and_project",
    )(place, *quarters, both)


def shards(stiffness_tiles, tile_cols, send_rows, block, lower_bound, upper_bound):
    rows, nnz, tile, _ = stiffness_tiles.shape
    dof_total = block.shape[0] * lax.axis_size(DOF)
    ghosts = 2 * send_rows.shape[1]
    place = jnp.stack([lax.axis_index(M), lax.axis_index(C)]).astype(jnp.int32)
    layout = Plan(rows, nnz)
    bounds = (lower_bound, upper_bound)
    level_0 = block.T

    near, far = exchange(*pick_lists(place, send_rows, level_0, tile))
    tiles, local, ghost = stage(tile_cols.T, stiffness_tiles.reshape(rows * nnz, tile, tile), ghosts)

    def level(index, total, near, far, field, previous=None):
        return next_level(
            index, layout, place, ghost, send_rows, bounds, tiles, total, near, far, field, previous
        )

    total = local_sums(1, layout, local, tiles, level_0)
    level_1, near, far = level(1, total, near, far, level_0)
    near, far = exchange(near, far)
    total = local_sums(2, layout, local, tiles, level_1)
    filtered, near, far = level(2, total, near, far, level_1, level_0)
    near, far = exchange(near, far)
    partner = flipped(filtered, M, 1)
    total = local_sums(3, layout, local, tiles, filtered)
    keep, send, both = partial_sums(layout, place, ghost, tiles, total, near, far, filtered, partner)
    quarter = sum_over_chips(keep + flipped(send, C, 1))
    quarters = (quarter, flipped(quarter, C, 1), flipped(quarter, M, 1), flipped(quarter, (C, M), 3))
    basis, ritz = factor_and_project(place, quarters, both, dof_total)
    return (basis.T, ritz)


def solution(mesh):
    torus = Mesh(mesh.devices.reshape(4, 4, 4, 2, mesh.shape["mode"]), DOF + (M,))
    return jax.shard_map(
        shards,
        mesh=torus,
        in_specs=(P(DOF, None, None, None), P(DOF, None), P(DOF, None), P(DOF, M), P(), P()),
        out_specs=(P(DOF, M), P()),
        check_vma=False,
    )
```

```python
import jax
import jax.numpy as jnp
from jax import lax
from jax.experimental import pallas as pl
from jax.experimental.pallas import tpu as pltpu
from jax.sharding import Mesh
from jax.sharding import PartitionSpec as P

Z, X, Y, C, M = "dof_z", "dof_x", "dof_y", "dof_c", "mode"
DOF = (Z, X, Y, C)
VMEM = pl.BlockSpec(memory_space=pltpu.VMEM)
SMEM = pl.BlockSpec(memory_space=pltpu.SMEM)
HBM = pl.BlockSpec(memory_space=pltpu.HBM)
NT = (((1,), (1,)), ((), ()))
GROUP = 8


def params(mib):
    return pltpu.CompilerParams(vmem_limit_bytes=mib << 20)


def shape(dims, dtype):
    return jax.ShapeDtypeStruct(dims, dtype)


def flipped(block, axis, bits):
    return lax.ppermute(block, axis, [(i, i ^ bits) for i in range(lax.axis_size(axis))])


def swapped_between_chips(block):
    count = lax.axis_size(DOF)
    pairs = [(i, i + 1) for i in range(1, count - 1, 2)]
    return lax.ppermute(block, DOF, pairs + [(b, a) for a, b in pairs])


def columns(index, tile):
    return pl.ds(pl.multiple_of(index * tile, tile), tile)


def pick_lists(place, send_rows, field, tile):
    modes, width = field.shape
    count = send_rows.shape[1]
    part = shape((modes, count * tile), field.dtype)

    def kernel(place, send, field, held, far, near, rows, sems):
        copies = [
            pltpu.make_async_copy(send, rows, sems.at[0]),
            pltpu.make_async_copy(field, held, sems.at[1]),
        ]
        for copy in copies:
            copy.start()
        for copy in copies:
            copy.wait()
        core = place[1]
        for slot in range(count):
            here = slice(slot * tile, (slot + 1) * tile)
            far[:, here] = held[:, columns(rows[core, slot], tile)]
            near[:, here] = held[:, columns(rows[1 - core, slot], tile)]

    return pl.pallas_call(
        kernel,
        out_shape=(shape(field.shape, field.dtype), part, part),
        in_specs=[SMEM, HBM, HBM],
        out_specs=(VMEM,) * 3,
        scratch_shapes=[pltpu.SMEM(send_rows.shape, jnp.int32), pltpu.SemaphoreType.DMA((2,))],
        compiler_params=params(4),
        name="pick_lists",
    )(
        place,
        pltpu.with_memory_space_constraint(send_rows, pltpu.HBM),
        pltpu.with_memory_space_constraint(field, pltpu.HBM),
    )


def make_plan(place, send_rows, tile_cols, ghosts):
    nnz, rows = tile_cols.shape
    count = send_rows.shape[1]

    def kernel(place, send, cols, table, order, taken):
        code = [cols[k : k + 1, :] for k in range(nnz)]
        local = [(one < rows).astype(jnp.int32) for one in code]
        locals_before, total = [], jnp.zeros_like(code[0])
        for one in local:
            locals_before.append(total)
            total = total + one
        position = [
            jnp.where(local[k] == 1, locals_before[k], total + k - locals_before[k]) for k in range(nnz)
        ]
        for p in range(nnz):
            source, entry = jnp.zeros_like(total), jnp.zeros_like(total)
            for k in range(nnz):
                source = jnp.where(position[k] == p, code[k], source)
                entry = jnp.where(position[k] == p, k, entry)
            table[p : p + 1, :] = jnp.where(p < total, source, rows)
            table[nnz + p : nnz + p + 1, :] = jnp.where(p < total, ghosts, source - rows)
            table[2 * nnz + p : 2 * nnz + p + 1, :] = entry
        table[3 * nnz : 3 * nnz + 1, :] = nnz // 2 - (total >> 1)

        core = place[1]
        for row in range(rows):
            taken[row] = 0
        for slot in range(count):
            for start, which in ((0, core), (count, 1 - core)):
                row = send[which, slot]
                taken[row] = 1
                order[start + slot] = row
        at = jnp.int32(2 * count)
        for row in range(rows):
            order[at] = row
            at = at + 1 - taken[row]
        for i in range(GROUP):
            order[at + i] = order[0]
        order[2 * rows] = (at + GROUP - 1) // GROUP

    return pl.pallas_call(
        kernel,
        out_shape=(shape((3 * nnz + 2, rows), jnp.int32), shape((2 * rows + 8,), jnp.int32)),
        in_specs=[SMEM, SMEM, VMEM],
        out_specs=(VMEM, SMEM),
        scratch_shapes=[pltpu.SMEM((rows,), jnp.int32)],
        compiler_params=params(4),
        name="make_plan",
    )(place, send_rows, tile_cols)


def local_rows(table, tiles, sources, total, step, nnz):
    tile = tiles.shape[1]
    for u in range(GROUP):
        row = step * GROUP + u
        source = [sources[:, columns(table[p, row], tile)] for p in range(nnz - 2)]
        stored = [tiles[row * nnz + table[2 * nnz + p, row]] for p in range(nnz - 2)]
        total[:, columns(row, tile)] = lax.dot_general(
            jnp.concatenate(source, axis=1), jnp.concatenate(stored, axis=1), NT, preferred_element_type=jnp.float32
        )


def fill_sources(field, sources):
    width = field.shape[1]
    sources[:, :width] = field[...]
    sources[:, width:] = jnp.zeros((field.shape[0], sources.shape[1] - width), sources.dtype)


def stage_and_sum(table, tiles, field, rows, nnz):
    modes, width = field.shape
    tile = tiles.shape[1]
    per_chunk = GROUP // 2 * nnz
    chunks = rows * nnz // per_chunk

    def kernel(table, tiles, field, staged, total, sources, sems):
        def chunk(i):
            here = pl.ds(i * per_chunk, per_chunk)
            return pltpu.make_async_copy(tiles.at[here], staged.at[here], sems.at[i])

        for i in range(chunks):
            chunk(i).start()
        fill_sources(field, sources)

        def step(i, carry):
            chunk(2 * i).wait()
            chunk(2 * i + 1).wait()
            local_rows(table, staged, sources, total, i, nnz)
            return carry

        lax.fori_loop(0, rows // GROUP, step, 0)

    return pl.pallas_call(
        kernel,
        out_shape=(shape(tiles.shape, tiles.dtype), shape((modes, width), jnp.float32)),
        in_specs=[SMEM, HBM, VMEM],
        out_specs=(VMEM, VMEM),
        scratch_shapes=[pltpu.VMEM((modes, width + tile), field.dtype), pltpu.SemaphoreType.DMA((chunks,))],
        compiler_params=params(8),
        cost_estimate=pl.CostEstimate(flops=2 * tiles.size * modes, bytes_accessed=2 * tiles.size, transcendentals=0),
        name="stage_and_sum",
    )(table, pltpu.with_memory_space_constraint(tiles, pltpu.HBM), field)


def local_sums(level, table, tiles, field, rows, nnz):
    modes, width = field.shape
    tile = tiles.shape[1]

    def kernel(table, tiles, field, total, sources):
        fill_sources(field, sources)

        def step(i, carry):
            local_rows(table, tiles, sources, total, i, nnz)
            return carry

        lax.fori_loop(0, rows // GROUP, step, 0)

    return pl.pallas_call(
        kernel,
        out_shape=shape((modes, width), jnp.float32),
        in_specs=[SMEM, VMEM, VMEM],
        out_specs=VMEM,
        scratch_shapes=[pltpu.VMEM((modes, width + tile), field.dtype)],
        compiler_params=params(8),
        cost_estimate=pl.CostEstimate(flops=tiles.size * modes // 8, bytes_accessed=0, transcendentals=0),
        name=f"local_sums_{level}",
    )(table, tiles, field)


def fill_ghosts(core, near, far, ghosts):
    width = near.shape[1]
    ghosts[:, columns(1 - core, width)] = near[...]
    ghosts[:, columns(core, width)] = far[...]
    ghosts[:, 2 * width :] = jnp.zeros((near.shape[0], ghosts.shape[1] - 2 * width), ghosts.dtype)


def ghost_rows(table, order, tiles, ghosts, partial, first, nnz):
    tile = tiles.shape[1]
    rows = [first + u if order is None else order[first + u] for u in range(GROUP)]
    most = table[3 * nnz, rows[0]]
    for row in rows[1:]:
        most = jnp.maximum(most, table[3 * nnz, row])

    def add(q):
        for u, row in enumerate(rows):
            source = [ghosts[:, columns(table[nnz + 2 * q + i, row], tile)] for i in range(2)]
            stored = [tiles[row * nnz + table[2 * nnz + 2 * q + i, row]] for i in range(2)]
            product = lax.dot_general(
                jnp.concatenate(source, axis=1),
                jnp.concatenate(stored, axis=1),
                NT,
                preferred_element_type=jnp.float32,
            )
            here = slice(u * tile, (u + 1) * tile)
            partial[:, here] = product if q == nnz // 2 - 1 else partial[:, here] + product

    for q in reversed(range(nnz // 2)):
        if q == nnz // 2 - 1:
            add(q)
        else:
            pl.when(most >= nnz // 2 - q)(lambda q=q: add(q))
    return rows


def level_rows(level, bounds, rows, total, partial, field, previous, store):
    lower, upper = bounds
    modes, tile = field.shape[0], partial.shape[1] // GROUP
    center = (upper[0] + lower[0]) * 0.5
    factor = 1.0 / jnp.full((modes, tile), (upper[0] - lower[0]) * 0.5, jnp.float32)
    for u, row in enumerate(rows):
        here = columns(row, tile)
        value = total[:, here] + partial[:, u * tile : (u + 1) * tile]
        value = (value - center * field[:, here].astype(jnp.float32)) * factor
        if level == 2:
            value = 2.0 * value - previous[:, here].astype(jnp.float32)
        store(u, row, value.astype(field.dtype))


def next_lists(level, nnz, place, table, order, bounds, tiles, total, near, far, field, previous):
    tile = tiles.shape[1]

    def kernel(place, table, order, lower, upper, tiles, total, near, far, field, *rest):
        if level == 2:
            previous, *rest = rest
        else:
            previous = None
        new_far, new_near, ghosts, partial = rest
        fill_ghosts(place[1], near, far, ghosts)
        for out, first in ((new_far, 0), (new_near, GROUP)):
            rows = ghost_rows(table, order, tiles, ghosts, partial, first, nnz)

            def store(u, row, value, out=out):
                out[:, u * tile : (u + 1) * tile] = value

            level_rows(level, (lower, upper), rows, total, partial, field, previous, store)

    operands = [place, table, order, *bounds, tiles, total, near, far, field] + [previous] * (level == 2)
    return pl.pallas_call(
        kernel,
        out_shape=(shape(far.shape, far.dtype),) * 2,
        in_specs=[SMEM] * 5 + [VMEM] * (len(operands) - 5),
        out_specs=(VMEM,) * 2,
        scratch_shapes=[
            pltpu.VMEM((far.shape[0], 2 * far.shape[1] + tile), far.dtype),
            pltpu.VMEM((far.shape[0], GROUP * tile), jnp.float32),
        ],
        compiler_params=params(8),
        name=f"next_lists_{level}",
    )(*operands)


def next_level(level, nnz, place, table, order, bounds, tiles, total, near, far, field, previous, new_far, new_near):
    modes, width = field.shape
    tile = tiles.shape[1]

    def kernel(place, table, order, lower, upper, tiles, total, near, far, field, new_far, new_near, *rest):
        if level == 2:
            previous, *rest = rest
        else:
            previous = None
        out, ghosts, partial = rest
        fill_ghosts(place[1], near, far, ghosts)
        for held, first in ((new_far, 0), (new_near, GROUP)):
            for u in range(GROUP):
                out[:, columns(order[first + u], tile)] = held[:, u * tile : (u + 1) * tile]

        def store(u, row, value):
            out[:, columns(row, tile)] = value

        def step(i, carry):
            rows = ghost_rows(table, order, tiles, ghosts, partial, i * GROUP, nnz)
            level_rows(level, (lower, upper), rows, total, partial, field, previous, store)
            return carry

        lax.fori_loop(2, order[2 * width // tile], step, 0)

    operands = [place, table, order, *bounds, tiles, total, near, far, field, new_far, new_near]
    operands += [previous] * (level == 2)
    return pl.pallas_call(
        kernel,
        out_shape=shape(field.shape, field.dtype),
        in_specs=[SMEM] * 5 + [VMEM] * (len(operands) - 5),
        out_specs=VMEM,
        scratch_shapes=[
            pltpu.VMEM((modes, 2 * far.shape[1] + tile), far.dtype),
            pltpu.VMEM((modes, GROUP * tile), jnp.float32),
        ],
        compiler_params=params(8),
        cost_estimate=pl.CostEstimate(flops=tiles.size * modes, bytes_accessed=2 * tiles.size, transcendentals=0),
        name=f"next_level_{level}",
    )(*operands)


def image_rows(nnz, place, table, tiles, total, near, far):
    modes, width = total.shape
    tile = tiles.shape[1]

    def kernel(place, table, tiles, total, near, far, out, ghosts, partial):
        fill_ghosts(place[1], near, far, ghosts)

        def step(i, carry):
            rows = ghost_rows(table, None, tiles, ghosts, partial, i * GROUP, nnz)
            for u, row in enumerate(rows):
                here = columns(row, tile)
                out[:, here] = (total[:, here] + partial[:, u * tile : (u + 1) * tile]).astype(out.dtype)
            return carry

        lax.fori_loop(0, width // tile // GROUP, step, 0)

    return pl.pallas_call(
        kernel,
        out_shape=shape((modes, width), near.dtype),
        in_specs=[SMEM] * 2 + [VMEM] * 4,
        out_specs=VMEM,
        scratch_shapes=[
            pltpu.VMEM((modes, 2 * near.shape[1] + tile), near.dtype),
            pltpu.VMEM((modes, GROUP * tile), jnp.float32),
        ],
        compiler_params=params(8),
        cost_estimate=pl.CostEstimate(flops=20 * tiles.size * modes, bytes_accessed=2 * tiles.size, transcendentals=0),
        name="image_rows",
    )(place, table, tiles, total, near, far)


def partial_sums(place, own, partner, image):
    modes, width = own.shape
    product = shape((modes, 2 * modes), jnp.float32)

    def kernel(place, own, partner, image, keep, send, both, left):
        mode, core = place[0], place[1]
        both[columns(mode, modes), :] = own[...]
        both[columns(1 - mode, modes), :] = partner[...]
        left[columns(core, modes), :] = own[...]
        left[columns(1 - core, modes), :] = image[...]
        sums = lax.dot_general(left[...], both[...], NT, preferred_element_type=jnp.float32)
        keep[...] = sums[:modes]
        send[...] = sums[modes:]

    return pl.pallas_call(
        kernel,
        out_shape=(product, product, shape((2 * modes, width), own.dtype)),
        in_specs=[SMEM] + [VMEM] * 3,
        out_specs=(VMEM,) * 3,
        scratch_shapes=[pltpu.VMEM((2 * modes, width), own.dtype)],
        compiler_params=params(12),
        name="partial_sums",
    )(place, own, partner, image)


def sum_over_chips(value):
    for axis in (X, Y, Z):
        others = [flipped(value, axis, bits) for bits in (1, 2, 3)]
        value = (value + others[0]) + (others[1] + others[2])
    return value


def spread(block, lane):
    return jnp.broadcast_to(block[:, lane : lane + 1], block.shape)


def eliminated(blocks):
    rows, size = blocks[0].shape
    sub = lax.broadcasted_iota(jnp.int32, (rows, size), 0)
    lane = lax.broadcasted_iota(jnp.int32, (rows, size), 1)
    blocks = list(blocks)
    for b in range(len(blocks)):
        first = rows * b
        row = [jnp.broadcast_to(blocks[b][s : s + 1, :], (rows, size)) for s in range(rows)]
        d = {(t, s): spread(row[t], first + s) for t in range(rows) for s in range(t + 1)}
        unit = [row[s] + (lane == first + s).astype(jnp.float32) for s in range(rows)]
        ratio, reciprocal = {}, []
        for s in range(rows):
            reciprocal.append(1.0 / d[s, s])
            for t in range(s + 1, rows):
                ratio[t, s] = d[t, s] * reciprocal[s]
            for t in range(s + 1, rows):
                for q in range(s + 1, t + 1):
                    d[t, q] = d[t, q] - ratio[t, s] * d[q, s]
                unit[t] = unit[t] - ratio[t, s] * unit[s]
        solved = [None] * rows
        for s in reversed(range(rows)):
            value = unit[s] * reciprocal[s]
            for t in range(s + 1, rows):
                value = value - ratio[t, s] * solved[t]
            solved[s] = value
        for k in range(b + 1, len(blocks)):
            value = blocks[k]
            for s in range(rows):
                value = value - spread(blocks[k], first + s) * solved[s]
            blocks[k] = value
        value = blocks[b]
        for s in range(rows):
            value = jnp.where(sub == s, unit[s] - (lane == first + s).astype(jnp.float32), value)
        blocks[b] = value
    return blocks


def factor_and_project(place, quarters, both, dof_total):
    modes, width = both.shape[0] // 2, both.shape[1]
    size = 2 * modes

    def kernel(place, own, other_core, other_mode, last, both, basis, ritz, sums, inverse):
        mode, core = place[0], place[1]
        for part, c, m in (
            (own, core, mode),
            (other_core, 1 - core, mode),
            (other_mode, core, 1 - mode),
            (last, 1 - core, 1 - mode),
        ):
            sums[columns(2 * c + m, modes), :] = part[...] / dof_total
        blocks = eliminated([sums[i : i + 8, :] for i in range(0, size, 8)])
        matrix = jnp.concatenate(blocks, axis=0)
        sub = lax.broadcasted_iota(jnp.int32, (size, size), 0)
        lane = lax.broadcasted_iota(jnp.int32, (size, size), 1)
        pivots = jnp.sum(jnp.where(sub == lane, matrix, 0.0), axis=1, keepdims=True)
        lower = jnp.where(lane < sub, matrix, jnp.where(lane == sub, 1.0, 0.0)) * lax.rsqrt(pivots)
        inverse[...] = lower
        left = inverse[columns(mode, modes), :].astype(both.dtype)
        basis[...] = jnp.dot(left, both[...], preferred_element_type=jnp.float32).astype(basis.dtype)
        half = lax.dot_general(
            lower, sums[size:, :], NT, precision=lax.Precision.HIGHEST, preferred_element_type=jnp.float32
        )
        ritz[...] = lax.dot_general(
            half, lower, NT, precision=lax.Precision.HIGHEST, preferred_element_type=jnp.float32
        )

    return pl.pallas_call(
        kernel,
        out_shape=(shape((modes, width), both.dtype), shape((size, size), jnp.float32)),
        in_specs=[SMEM] + [VMEM] * 5,
        out_specs=(VMEM, VMEM),
        scratch_shapes=[pltpu.VMEM((2 * size, size), jnp.float32), pltpu.VMEM((size, size), jnp.float32)],
        compiler_params=params(12),
        name="factor_and_project",
    )(place, *quarters, both)


def shards(stiffness_tiles, tile_cols, send_rows, block, lower_bound, upper_bound):
    rows, nnz, tile, _ = stiffness_tiles.shape
    dof_total = block.shape[0] * lax.axis_size(DOF)
    ghosts = 2 * send_rows.shape[1]
    place = jnp.stack([lax.axis_index(M), lax.axis_index(C)]).astype(jnp.int32)
    bounds = (lower_bound, upper_bound)

    level_0, far, near = pick_lists(place, send_rows, block.T, tile)
    far, near = swapped_between_chips(far), flipped(near, C, 1)
    table, order = make_plan(place, send_rows, tile_cols.T, ghosts)
    tiles, total = stage_and_sum(table, stiffness_tiles.reshape(rows * nnz, tile, tile), level_0, rows, nnz)

    def level(index, total, near, far, field, previous=None):
        known = (nnz, place, table, order, bounds, tiles, total, near, far, field, previous)
        new_far, new_near = next_lists(index, *known)
        arrived = flipped(new_near, C, 1), swapped_between_chips(new_far)
        field = next_level(index, *known, new_far, new_near)
        return field, *arrived, local_sums(index + 1, table, tiles, field, rows, nnz)

    level_1, near, far, total = level(1, total, near, far, level_0)
    filtered, near, far, total = level(2, total, near, far, level_1, level_0)
    partner = flipped(filtered, M, 1)
    image = image_rows(nnz, place, table, tiles, total, near, far)
    keep, send, both = partial_sums(place, filtered, partner, image)
    quarter = sum_over_chips(keep + flipped(send, C, 1))
    quarters = (quarter, flipped(quarter, C, 1), flipped(quarter, M, 1), flipped(quarter, (C, M), 3))
    basis, ritz = factor_and_project(place, quarters, both, dof_total)
    return (basis.T, ritz)


def solution(mesh):
    torus = Mesh(mesh.devices.reshape(4, 4, 4, 2, mesh.shape["mode"]), DOF + (M,))
    return jax.shard_map(
        shards,
        mesh=torus,
        in_specs=(P(DOF, None, None, None), P(DOF, None), P(DOF, None), P(DOF, M), P(), P()),
        out_specs=(P(DOF, M), P()),
        check_vma=False,
    )
```

```python
import jax
import jax.numpy as jnp
from jax import lax
from jax.experimental import pallas as pl
from jax.experimental.pallas import tpu as pltpu
from jax.sharding import Mesh
from jax.sharding import PartitionSpec as P

Z, X, Y, C, M = "dof_z", "dof_x", "dof_y", "dof_c", "mode"
DOF = (Z, X, Y, C)
VMEM = pl.BlockSpec(memory_space=pltpu.VMEM)
SMEM = pl.BlockSpec(memory_space=pltpu.SMEM)
HBM = pl.BlockSpec(memory_space=pltpu.HBM)
NT = (((1,), (1,)), ((), ()))
GROUP = 8


def params(mib):
    return pltpu.CompilerParams(vmem_limit_bytes=mib << 20)


def shape(dims, dtype):
    return jax.ShapeDtypeStruct(dims, dtype)


def flipped(block, axis, bits):
    return lax.ppermute(block, axis, [(i, i ^ bits) for i in range(lax.axis_size(axis))])


def swapped_between_chips(block):
    count = lax.axis_size(DOF)
    pairs = [(i, i + 1) for i in range(1, count - 1, 2)]
    return lax.ppermute(block, DOF, pairs + [(b, a) for a, b in pairs])


def columns(index, tile):
    return pl.ds(pl.multiple_of(index * tile, tile), tile)


def pick_lists(place, send_rows, field, tile):
    modes, width = field.shape
    count = send_rows.shape[1]
    part = shape((modes, count * tile), field.dtype)

    def kernel(place, send, field, held, far, near, rows, sems):
        copies = [
            pltpu.make_async_copy(send, rows, sems.at[0]),
            pltpu.make_async_copy(field, held, sems.at[1]),
        ]
        for copy in copies:
            copy.start()
        for copy in copies:
            copy.wait()
        core = place[1]
        for slot in range(count):
            here = slice(slot * tile, (slot + 1) * tile)
            far[:, here] = held[:, columns(rows[core, slot], tile)]
            near[:, here] = held[:, columns(rows[1 - core, slot], tile)]

    return pl.pallas_call(
        kernel,
        out_shape=(shape(field.shape, field.dtype), part, part),
        in_specs=[SMEM, HBM, HBM],
        out_specs=(VMEM,) * 3,
        scratch_shapes=[pltpu.SMEM(send_rows.shape, jnp.int32), pltpu.SemaphoreType.DMA((2,))],
        compiler_params=params(4),
        name="pick_lists",
    )(
        place,
        pltpu.with_memory_space_constraint(send_rows, pltpu.HBM),
        pltpu.with_memory_space_constraint(field, pltpu.HBM),
    )


def make_plan(core, code, send, table, order, taken):
    nnz, rows, count = len(code), code[0].shape[1], send.shape[1]
    local = [(one < rows).astype(jnp.int32) for one in code]
    locals_before, total = [], jnp.zeros_like(code[0])
    for one in local:
        locals_before.append(total)
        total = total + one
    position = [jnp.where(local[k] == 1, locals_before[k], total + k - locals_before[k]) for k in range(nnz)]
    for p in range(nnz):
        source, entry = jnp.zeros_like(total), jnp.zeros_like(total)
        for k in range(nnz):
            source = jnp.where(position[k] == p, code[k], source)
            entry = jnp.where(position[k] == p, k, entry)
        table[p : p + 1, :] = jnp.where(p < total, source, rows)
        table[nnz + p : nnz + p + 1, :] = jnp.where(p < total, 2 * count, source - rows)
        table[2 * nnz + p : 2 * nnz + p + 1, :] = entry
    table[3 * nnz : 3 * nnz + 1, :] = nnz // 2 - (total >> 1)

    for row in range(rows):
        taken[row] = 0
    for slot in range(count):
        for start, which in ((0, core), (count, 1 - core)):
            row = send[which, slot]
            taken[row] = 1
            order[start + slot] = row
    at = jnp.int32(2 * count)
    for row in range(rows):
        order[at] = row
        at = at + 1 - taken[row]
    for i in range(GROUP):
        order[at + i] = order[0]
    order[2 * rows] = (at + GROUP - 1) // GROUP


def local_rows(table, tiles, sources, total, step, nnz):
    for u in range(GROUP):
        row = step * GROUP + u
        total[:, columns(row, tiles.shape[1])] = summed(table, tiles, sources, row, 0, range(nnz - 2), nnz)


def summed(table, tiles, sources, row, kind, positions, nnz):
    tile = tiles.shape[1]
    source = [sources[:, columns(table[kind * nnz + p, row], tile)] for p in positions]
    stored = [tiles[row * nnz + table[2 * nnz + p, row]] for p in positions]
    return jnp.dot(
        jnp.concatenate(source, axis=1), jnp.concatenate(stored, axis=0), preferred_element_type=jnp.float32
    )


def fill_sources(field, sources):
    width = field.shape[1]
    sources[:, :width] = field[...]
    sources[:, width:] = jnp.zeros((field.shape[0], sources.shape[1] - width), sources.dtype)


def stage_and_sum(place, send_rows, tile_cols, tiles, field):
    modes, width = field.shape
    nnz, rows = tile_cols.shape
    tile = tiles.shape[1]
    per_chunk = GROUP // 2 * nnz
    chunks = rows * nnz // per_chunk
    table_shape = (3 * nnz + 2, rows)

    def kernel(place, send_hbm, cols_hbm, tiles, field, staged, total, table, order, *scratch):
        sources, raw, cols, made, send, taken, sems, small = scratch

        def chunk(i):
            here = pl.ds(i * per_chunk, per_chunk)
            return pltpu.make_async_copy(tiles.at[here], raw.at[here], sems.at[i])

        lists = [
            pltpu.make_async_copy(send_hbm, send, small.at[0]),
            pltpu.make_async_copy(cols_hbm, cols, small.at[1]),
        ]
        for copy in lists:
            copy.start()
        for i in range(chunks):
            chunk(i).start()
        fill_sources(field, sources)
        for copy in lists:
            copy.wait()
        make_plan(place[1], [cols[k : k + 1, :] for k in range(nnz)], send, made, order, taken)
        copy = pltpu.make_async_copy(made, table, small.at[2])
        copy.start()
        copy.wait()

        def step(i, carry):
            chunk(2 * i).wait()
            chunk(2 * i + 1).wait()

            def turn(j, carry):
                for u in range(GROUP):
                    at = i * 2 * per_chunk + j * GROUP + u
                    staged[at] = raw[at].T
                return carry

            lax.fori_loop(0, 2 * per_chunk // GROUP, turn, 0)
            local_rows(table, staged, sources, total, i, nnz)
            return carry

        lax.fori_loop(0, rows // GROUP, step, 0)

    def in_hbm(array):
        return pltpu.with_memory_space_constraint(array, pltpu.HBM)

    return pl.pallas_call(
        kernel,
        out_shape=(
            shape(tiles.shape, tiles.dtype),
            shape((modes, width), jnp.float32),
            shape(table_shape, jnp.int32),
            shape((2 * rows + 8,), jnp.int32),
        ),
        in_specs=[SMEM, HBM, HBM, HBM, VMEM],
        out_specs=(VMEM, VMEM, SMEM, SMEM),
        scratch_shapes=[
            pltpu.VMEM((modes, width + tile), field.dtype),
            pltpu.VMEM(tiles.shape, tiles.dtype),
            pltpu.VMEM(tile_cols.shape, jnp.int32),
            pltpu.VMEM(table_shape, jnp.int32),
            pltpu.SMEM(send_rows.shape, jnp.int32),
            pltpu.SMEM((rows,), jnp.int32),
            pltpu.SemaphoreType.DMA((chunks,)),
            pltpu.SemaphoreType.DMA((3,)),
        ],
        compiler_params=params(16),
        cost_estimate=pl.CostEstimate(flops=2 * tiles.size * modes, bytes_accessed=2 * tiles.size, transcendentals=0),
        name="stage_and_sum",
    )(place, in_hbm(send_rows), in_hbm(tile_cols), in_hbm(tiles), field)


def local_sums(level, table, tiles, field, rows, nnz):
    modes, width = field.shape
    tile = tiles.shape[1]

    def kernel(table, tiles, field, total, sources):
        fill_sources(field, sources)

        def step(i, carry):
            local_rows(table, tiles, sources, total, i, nnz)
            return carry

        lax.fori_loop(0, rows // GROUP, step, 0)

    return pl.pallas_call(
        kernel,
        out_shape=shape((modes, width), jnp.float32),
        in_specs=[SMEM, VMEM, VMEM],
        out_specs=VMEM,
        scratch_shapes=[pltpu.VMEM((modes, width + tile), field.dtype)],
        compiler_params=params(8),
        cost_estimate=pl.CostEstimate(flops=tiles.size * modes // 8, bytes_accessed=0, transcendentals=0),
        name=f"local_sums_{level}",
    )(table, tiles, field)


def fill_ghosts(core, near, far, ghosts):
    width = near.shape[1]
    ghosts[:, columns(1 - core, width)] = near[...]
    ghosts[:, columns(core, width)] = far[...]
    ghosts[:, 2 * width :] = jnp.zeros((near.shape[0], ghosts.shape[1] - 2 * width), ghosts.dtype)


def ghost_rows(table, order, tiles, ghosts, partial, first, nnz):
    tile = tiles.shape[1]
    rows = [first + u if order is None else order[first + u] for u in range(GROUP)]
    most = table[3 * nnz, rows[0]]
    for row in rows[1:]:
        most = jnp.maximum(most, table[3 * nnz, row])
    usual = 3
    for u, row in enumerate(rows):
        positions = range(nnz - 2 * usual, nnz)
        partial[:, u * tile : (u + 1) * tile] = summed(table, tiles, ghosts, row, 1, positions, nnz)

    @pl.when(most > usual)
    def _():
        for u, row in enumerate(rows):
            here = slice(u * tile, (u + 1) * tile)
            partial[:, here] = partial[:, here] + summed(table, tiles, ghosts, row, 1, range(nnz - 2 * usual), nnz)

    return rows


def level_rows(level, bounds, rows, total, partial, field, previous, store):
    lower, upper = bounds
    modes, tile = field.shape[0], partial.shape[1] // GROUP
    center = (upper[0] + lower[0]) * 0.5
    factor = 1.0 / jnp.full((modes, tile), (upper[0] - lower[0]) * 0.5, jnp.float32)
    for u, row in enumerate(rows):
        here = columns(row, tile)
        value = total[:, here] + partial[:, u * tile : (u + 1) * tile]
        value = (value - center * field[:, here].astype(jnp.float32)) * factor
        if level == 2:
            value = 2.0 * value - previous[:, here].astype(jnp.float32)
        store(u, row, value.astype(field.dtype))


def next_lists(level, nnz, place, table, order, bounds, tiles, total, near, far, field, previous):
    tile = tiles.shape[1]

    def kernel(place, table, order, lower, upper, tiles, total, near, far, field, *rest):
        if level == 2:
            previous, *rest = rest
        else:
            previous = None
        new_far, new_near, ghosts, partial = rest
        fill_ghosts(place[1], near, far, ghosts)
        for out, first in ((new_far, 0), (new_near, GROUP)):
            rows = ghost_rows(table, order, tiles, ghosts, partial, first, nnz)

            def store(u, row, value, out=out):
                out[:, u * tile : (u + 1) * tile] = value

            level_rows(level, (lower, upper), rows, total, partial, field, previous, store)

    operands = [place, table, order, *bounds, tiles, total, near, far, field] + [previous] * (level == 2)
    return pl.pallas_call(
        kernel,
        out_shape=(shape(far.shape, far.dtype),) * 2,
        in_specs=[SMEM] * 5 + [VMEM] * (len(operands) - 5),
        out_specs=(VMEM,) * 2,
        scratch_shapes=[
            pltpu.VMEM((far.shape[0], 2 * far.shape[1] + tile), far.dtype),
            pltpu.VMEM((far.shape[0], GROUP * tile), jnp.float32),
        ],
        compiler_params=params(8),
        name=f"next_lists_{level}",
    )(*operands)


def next_level(level, nnz, place, table, order, bounds, tiles, total, near, far, field, previous, new_far, new_near):
    modes, width = field.shape
    tile = tiles.shape[1]

    def kernel(place, table, order, lower, upper, tiles, total, near, far, field, new_far, new_near, *rest):
        if level == 2:
            previous, *rest = rest
        else:
            previous = None
        out, ghosts, partial = rest
        fill_ghosts(place[1], near, far, ghosts)
        for held, first in ((new_far, 0), (new_near, GROUP)):
            for u in range(GROUP):
                out[:, columns(order[first + u], tile)] = held[:, u * tile : (u + 1) * tile]

        def store(u, row, value):
            out[:, columns(row, tile)] = value

        def step(i, carry):
            rows = ghost_rows(table, order, tiles, ghosts, partial, i * GROUP, nnz)
            level_rows(level, (lower, upper), rows, total, partial, field, previous, store)
            return carry

        lax.fori_loop(2, order[2 * width // tile], step, 0)

    operands = [place, table, order, *bounds, tiles, total, near, far, field, new_far, new_near]
    operands += [previous] * (level == 2)
    return pl.pallas_call(
        kernel,
        out_shape=shape(field.shape, field.dtype),
        in_specs=[SMEM] * 5 + [VMEM] * (len(operands) - 5),
        out_specs=VMEM,
        scratch_shapes=[
            pltpu.VMEM((modes, 2 * far.shape[1] + tile), far.dtype),
            pltpu.VMEM((modes, GROUP * tile), jnp.float32),
        ],
        compiler_params=params(8),
        cost_estimate=pl.CostEstimate(flops=tiles.size * modes, bytes_accessed=2 * tiles.size, transcendentals=0),
        name=f"next_level_{level}",
    )(*operands)


def image_rows(nnz, place, table, tiles, total, near, far):
    modes, width = total.shape
    tile = tiles.shape[1]

    def kernel(place, table, tiles, total, near, far, out, ghosts, partial):
        fill_ghosts(place[1], near, far, ghosts)

        def step(i, carry):
            rows = ghost_rows(table, None, tiles, ghosts, partial, i * GROUP, nnz)
            for u, row in enumerate(rows):
                here = columns(row, tile)
                out[:, here] = (total[:, here] + partial[:, u * tile : (u + 1) * tile]).astype(out.dtype)
            return carry

        lax.fori_loop(0, width // tile // GROUP, step, 0)

    return pl.pallas_call(
        kernel,
        out_shape=shape((modes, width), near.dtype),
        in_specs=[SMEM] * 2 + [VMEM] * 4,
        out_specs=VMEM,
        scratch_shapes=[
            pltpu.VMEM((modes, 2 * near.shape[1] + tile), near.dtype),
            pltpu.VMEM((modes, GROUP * tile), jnp.float32),
        ],
        compiler_params=params(8),
        cost_estimate=pl.CostEstimate(flops=20 * tiles.size * modes, bytes_accessed=2 * tiles.size, transcendentals=0),
        name="image_rows",
    )(place, table, tiles, total, near, far)


def partial_sums(place, own, partner, image):
    modes, width = own.shape
    product = shape((modes, 2 * modes), jnp.float32)

    def kernel(place, own, partner, image, keep, send, both, left):
        mode, core = place[0], place[1]
        both[columns(mode, modes), :] = own[...]
        both[columns(1 - mode, modes), :] = partner[...]
        left[columns(core, modes), :] = own[...]
        left[columns(1 - core, modes), :] = image[...]
        sums = lax.dot_general(left[...], both[...], NT, preferred_element_type=jnp.float32)
        keep[...] = sums[:modes]
        send[...] = sums[modes:]

    return pl.pallas_call(
        kernel,
        out_shape=(product, product, shape((2 * modes, width), own.dtype)),
        in_specs=[SMEM] + [VMEM] * 3,
        out_specs=(VMEM,) * 3,
        scratch_shapes=[pltpu.VMEM((2 * modes, width), own.dtype)],
        compiler_params=params(12),
        name="partial_sums",
    )(place, own, partner, image)


def sum_over_chips(value):
    for axis in (X, Y, Z):
        others = [flipped(value, axis, bits) for bits in (1, 2, 3)]
        value = (value + others[0]) + (others[1] + others[2])
    return value


def spread(block, lane):
    return jnp.broadcast_to(block[:, lane : lane + 1], block.shape)


def eliminated(blocks):
    rows, size = blocks[0].shape
    sub = lax.broadcasted_iota(jnp.int32, (rows, size), 0)
    lane = lax.broadcasted_iota(jnp.int32, (rows, size), 1)
    blocks = list(blocks)
    for b in range(len(blocks)):
        first = rows * b
        row = [jnp.broadcast_to(blocks[b][s : s + 1, :], (rows, size)) for s in range(rows)]
        d = {(t, s): spread(row[t], first + s) for t in range(rows) for s in range(t + 1)}
        unit = [row[s] + (lane == first + s).astype(jnp.float32) for s in range(rows)]
        ratio, reciprocal = {}, []
        for s in range(rows):
            reciprocal.append(1.0 / d[s, s])
            for t in range(s + 1, rows):
                ratio[t, s] = d[t, s] * reciprocal[s]
            for t in range(s + 1, rows):
                for q in range(s + 1, t + 1):
                    d[t, q] = d[t, q] - ratio[t, s] * d[q, s]
                unit[t] = unit[t] - ratio[t, s] * unit[s]
        solved = [None] * rows
        for s in reversed(range(rows)):
            value = unit[s] * reciprocal[s]
            for t in range(s + 1, rows):
                value = value - ratio[t, s] * solved[t]
            solved[s] = value
        for k in range(b + 1, len(blocks)):
            value = blocks[k]
            for s in range(rows):
                value = value - spread(blocks[k], first + s) * solved[s]
            blocks[k] = value
        value = blocks[b]
        for s in range(rows):
            value = jnp.where(sub == s, unit[s] - (lane == first + s).astype(jnp.float32), value)
        blocks[b] = value
    return blocks


def factor_and_project(place, quarters, both, dof_total):
    modes, width = both.shape[0] // 2, both.shape[1]
    size = 2 * modes

    def kernel(place, own, other_core, other_mode, last, both, basis, ritz, sums, inverse):
        mode, core = place[0], place[1]
        for part, c, m in (
            (own, core, mode),
            (other_core, 1 - core, mode),
            (other_mode, core, 1 - mode),
            (last, 1 - core, 1 - mode),
        ):
            sums[columns(2 * c + m, modes), :] = part[...] / dof_total
        blocks = eliminated([sums[i : i + 8, :] for i in range(0, size, 8)])
        matrix = jnp.concatenate(blocks, axis=0)
        sub = lax.broadcasted_iota(jnp.int32, (size, size), 0)
        lane = lax.broadcasted_iota(jnp.int32, (size, size), 1)
        pivots = jnp.sum(jnp.where(sub == lane, matrix, 0.0), axis=1, keepdims=True)
        lower = jnp.where(lane < sub, matrix, jnp.where(lane == sub, 1.0, 0.0)) * lax.rsqrt(pivots)
        inverse[...] = lower
        left = inverse[columns(mode, modes), :].astype(both.dtype)
        basis[...] = jnp.dot(left, both[...], preferred_element_type=jnp.float32).astype(basis.dtype)
        half = lax.dot_general(
            lower, sums[size:, :], NT, precision=lax.Precision.HIGHEST, preferred_element_type=jnp.float32
        )
        ritz[...] = lax.dot_general(
            half, lower, NT, precision=lax.Precision.HIGHEST, preferred_element_type=jnp.float32
        )

    return pl.pallas_call(
        kernel,
        out_shape=(shape((modes, width), both.dtype), shape((size, size), jnp.float32)),
        in_specs=[SMEM] + [VMEM] * 5,
        out_specs=(VMEM, VMEM),
        scratch_shapes=[pltpu.VMEM((2 * size, size), jnp.float32), pltpu.VMEM((size, size), jnp.float32)],
        compiler_params=params(12),
        name="factor_and_project",
    )(place, *quarters, both)


def shards(stiffness_tiles, tile_cols, send_rows, block, lower_bound, upper_bound):
    rows, nnz, tile, _ = stiffness_tiles.shape
    dof_total = block.shape[0] * lax.axis_size(DOF)
    place = jnp.stack([lax.axis_index(M), lax.axis_index(C)]).astype(jnp.int32)
    bounds = (lower_bound, upper_bound)

    level_0, far, near = pick_lists(place, send_rows, block.T, tile)
    far, near = swapped_between_chips(far), flipped(near, C, 1)
    tiles, total, table, order = stage_and_sum(
        place, send_rows, tile_cols.T, stiffness_tiles.reshape(rows * nnz, tile, tile), level_0
    )

    def level(index, total, near, far, field, previous=None):
        known = (nnz, place, table, order, bounds, tiles, total, near, far, field, previous)
        new_far, new_near = next_lists(index, *known)
        arrived = flipped(new_near, C, 1), swapped_between_chips(new_far)
        field = next_level(index, *known, new_far, new_near)
        return field, *arrived, local_sums(index + 1, table, tiles, field, rows, nnz)

    level_1, near, far, total = level(1, total, near, far, level_0)
    filtered, near, far, total = level(2, total, near, far, level_1, level_0)
    partner = flipped(filtered, M, 1)
    image = image_rows(nnz, place, table, tiles, total, near, far)
    keep, send, both = partial_sums(place, filtered, partner, image)
    quarter = sum_over_chips(keep + flipped(send, C, 1))
    quarters = (quarter, flipped(quarter, C, 1), flipped(quarter, M, 1), flipped(quarter, (C, M), 3))
    basis, ritz = factor_and_project(place, quarters, both, dof_total)
    return (basis.T, ritz)


def solution(mesh):
    torus = Mesh(mesh.devices.reshape(4, 4, 4, 2, mesh.shape["mode"]), DOF + (M,))
    return jax.shard_map(
        shards,
        mesh=torus,
        in_specs=(P(DOF, None, None, None), P(DOF, None), P(DOF, None), P(DOF, M), P(), P()),
        out_specs=(P(DOF, M), P()),
        check_vma=False,
    )
```

```python
import jax
import jax.numpy as jnp
from jax import lax
from jax.experimental import pallas as pl
from jax.experimental.pallas import tpu as pltpu
from jax.sharding import Mesh
from jax.sharding import PartitionSpec as P

Z, X, Y, C, M = "dof_z", "dof_x", "dof_y", "dof_c", "mode"
DOF = (Z, X, Y, C)
VMEM = pl.BlockSpec(memory_space=pltpu.VMEM)
SMEM = pl.BlockSpec(memory_space=pltpu.SMEM)
HBM = pl.BlockSpec(memory_space=pltpu.HBM)
NT = (((1,), (1,)), ((), ()))
GROUP = 8
IN_FLIGHT = 4


def params(mib):
    return pltpu.CompilerParams(vmem_limit_bytes=mib << 20)


def shape(dims, dtype):
    return jax.ShapeDtypeStruct(dims, dtype)


def flipped(block, axis, bits):
    return lax.ppermute(block, axis, [(i, i ^ bits) for i in range(lax.axis_size(axis))])


def swapped_between_chips(block):
    count = lax.axis_size(DOF)
    pairs = [(i, i + 1) for i in range(1, count - 1, 2)]
    return lax.ppermute(block, DOF, pairs + [(b, a) for a, b in pairs])


def columns(index, tile):
    return pl.ds(pl.multiple_of(index * tile, tile), tile)


def pick_lists(place, send_rows, field, tile):
    modes, width = field.shape
    count = send_rows.shape[1]
    part = shape((modes, count * tile), field.dtype)

    def kernel(place, send, field, held, far, near, rows, sems):
        copies = [
            pltpu.make_async_copy(send, rows, sems.at[0]),
            pltpu.make_async_copy(field, held, sems.at[1]),
        ]
        for copy in copies:
            copy.start()
        for copy in copies:
            copy.wait()
        core = place[1]
        for slot in range(count):
            here = slice(slot * tile, (slot + 1) * tile)
            far[:, here] = held[:, columns(rows[core, slot], tile)]
            near[:, here] = held[:, columns(rows[1 - core, slot], tile)]

    return pl.pallas_call(
        kernel,
        out_shape=(shape(field.shape, field.dtype), part, part),
        in_specs=[SMEM, HBM, HBM],
        out_specs=(VMEM,) * 3,
        scratch_shapes=[pltpu.SMEM(send_rows.shape, jnp.int32), pltpu.SemaphoreType.DMA((2,))],
        compiler_params=params(4),
        name="pick_lists",
    )(
        place,
        pltpu.with_memory_space_constraint(send_rows, pltpu.HBM),
        pltpu.with_memory_space_constraint(field, pltpu.HBM),
    )


def make_plan(core, code, send, table, order, taken):
    nnz, rows, count = len(code), code[0].shape[1], send.shape[1]
    local = [(one < rows).astype(jnp.int32) for one in code]
    locals_before, total = [], jnp.zeros_like(code[0])
    for one in local:
        locals_before.append(total)
        total = total + one
    position = [jnp.where(local[k] == 1, locals_before[k], total + k - locals_before[k]) for k in range(nnz)]
    for p in range(nnz):
        source, entry = jnp.zeros_like(total), jnp.zeros_like(total)
        for k in range(nnz):
            source = jnp.where(position[k] == p, code[k], source)
            entry = jnp.where(position[k] == p, k, entry)
        table[p : p + 1, :] = jnp.where(p < total, source, rows)
        table[nnz + p : nnz + p + 1, :] = jnp.where(p < total, 2 * count, source - rows)
        table[2 * nnz + p : 2 * nnz + p + 1, :] = entry
    table[3 * nnz : 3 * nnz + 1, :] = nnz // 2 - (total >> 1)

    for row in range(rows):
        taken[row] = 0
    for slot in range(count):
        for start, which in ((0, core), (count, 1 - core)):
            row = send[which, slot]
            taken[row] = 1
            order[start + slot] = row
    at = jnp.int32(2 * count)
    for row in range(rows):
        order[at] = row
        at = at + 1 - taken[row]
    for i in range(GROUP):
        order[at + i] = order[0]
    order[2 * rows] = (at + GROUP - 1) // GROUP


def local_row(table, tiles, sources, total, row, nnz):
    total[:, columns(row, tiles.shape[1])] = summed(table, tiles, sources, row, 0, range(nnz - 2), nnz)


def summed(table, tiles, sources, row, kind, positions, nnz):
    tile = tiles.shape[1]
    source = [sources[:, columns(table[kind * nnz + p, row], tile)] for p in positions]
    stored = [tiles[row * nnz + table[2 * nnz + p, row]] for p in positions]
    return jnp.dot(
        jnp.concatenate(source, axis=1), jnp.concatenate(stored, axis=0), preferred_element_type=jnp.float32
    )


def fill_sources(field, sources):
    width = field.shape[1]
    sources[:, :width] = field[...]
    sources[:, width:] = jnp.zeros((field.shape[0], sources.shape[1] - width), sources.dtype)


def stage_and_sum(place, send_rows, tile_cols, tiles, field):
    modes, width = field.shape
    nnz, rows = tile_cols.shape
    tile = tiles.shape[1]
    per_chunk = GROUP // 2 * nnz
    chunks = rows * nnz // per_chunk
    table_shape = (3 * nnz + 2, rows)

    def kernel(place, send_hbm, cols_hbm, tiles, field, staged, total, table, order, *scratch):
        sources, raw, cols, made, send, taken, sems, small = scratch

        def chunk(i):
            here = pl.ds(i * per_chunk, per_chunk)
            return pltpu.make_async_copy(tiles.at[here], raw.at[here], sems.at[i])

        lists = [
            pltpu.make_async_copy(send_hbm, send, small.at[0]),
            pltpu.make_async_copy(cols_hbm, cols, small.at[1]),
        ]
        for copy in lists:
            copy.start()
        for i in range(IN_FLIGHT):
            chunk(i).start()
        fill_sources(field, sources)
        def arrive(step):
            for i in (2 * step, 2 * step + 1):
                chunk(i).wait()

                @pl.when(i + IN_FLIGHT < chunks)
                def _():
                    chunk(i + IN_FLIGHT).start()

        def turn(step, u):
            for k in range(nnz):
                at = (step * GROUP + u) * nnz + k
                staged[at] = raw[at].T

        steps = rows // GROUP
        for copy in lists:
            copy.wait()
        arrive(0)
        for u in range(GROUP):
            turn(0, u)
        make_plan(place[1], [cols[k : k + 1, :] for k in range(nnz)], send, made, order, taken)
        copy = pltpu.make_async_copy(made, table, small.at[2])
        copy.start()
        copy.wait()

        def step(i, carry):
            arrive(i + 1)
            for u in range(GROUP):
                turn(i + 1, u)
                local_row(table, staged, sources, total, i * GROUP + u, nnz)
            return carry

        lax.fori_loop(0, steps - 1, step, 0)
        for u in range(GROUP):
            local_row(table, staged, sources, total, (steps - 1) * GROUP + u, nnz)

    def in_hbm(array):
        return pltpu.with_memory_space_constraint(array, pltpu.HBM)

    return pl.pallas_call(
        kernel,
        out_shape=(
            shape(tiles.shape, tiles.dtype),
            shape((modes, width), jnp.float32),
            shape(table_shape, jnp.int32),
            shape((2 * rows + 8,), jnp.int32),
        ),
        in_specs=[SMEM, HBM, HBM, HBM, VMEM],
        out_specs=(VMEM, VMEM, SMEM, SMEM),
        scratch_shapes=[
            pltpu.VMEM((modes, width + tile), field.dtype),
            pltpu.VMEM(tiles.shape, tiles.dtype),
            pltpu.VMEM(tile_cols.shape, jnp.int32),
            pltpu.VMEM(table_shape, jnp.int32),
            pltpu.SMEM(send_rows.shape, jnp.int32),
            pltpu.SMEM((rows,), jnp.int32),
            pltpu.SemaphoreType.DMA((chunks,)),
            pltpu.SemaphoreType.DMA((3,)),
        ],
        compiler_params=params(16),
        cost_estimate=pl.CostEstimate(flops=2 * tiles.size * modes, bytes_accessed=2 * tiles.size, transcendentals=0),
        name="stage_and_sum",
    )(place, in_hbm(send_rows), in_hbm(tile_cols), in_hbm(tiles), field)


def local_sums(level, table, tiles, field, rows, nnz):
    modes, width = field.shape
    tile = tiles.shape[1]

    def kernel(table, tiles, field, total, sources):
        fill_sources(field, sources)

        def step(i, carry):
            for u in range(GROUP):
                local_row(table, tiles, sources, total, i * GROUP + u, nnz)
            return carry

        lax.fori_loop(0, rows // GROUP, step, 0)

    return pl.pallas_call(
        kernel,
        out_shape=shape((modes, width), jnp.float32),
        in_specs=[SMEM, VMEM, VMEM],
        out_specs=VMEM,
        scratch_shapes=[pltpu.VMEM((modes, width + tile), field.dtype)],
        compiler_params=params(8),
        cost_estimate=pl.CostEstimate(flops=tiles.size * modes // 8, bytes_accessed=0, transcendentals=0),
        name=f"local_sums_{level}",
    )(table, tiles, field)


def fill_ghosts(core, near, far, ghosts):
    width = near.shape[1]
    ghosts[:, columns(1 - core, width)] = near[...]
    ghosts[:, columns(core, width)] = far[...]
    ghosts[:, 2 * width :] = jnp.zeros((near.shape[0], ghosts.shape[1] - 2 * width), ghosts.dtype)


def ghost_rows(table, order, tiles, ghosts, partial, first, nnz):
    tile = tiles.shape[1]
    rows = [first + u if order is None else order[first + u] for u in range(GROUP)]
    most = table[3 * nnz, rows[0]]
    for row in rows[1:]:
        most = jnp.maximum(most, table[3 * nnz, row])
    usual = 3
    for u, row in enumerate(rows):
        positions = range(nnz - 2 * usual, nnz)
        partial[:, u * tile : (u + 1) * tile] = summed(table, tiles, ghosts, row, 1, positions, nnz)

    @pl.when(most > usual)
    def _():
        for u, row in enumerate(rows):
            here = slice(u * tile, (u + 1) * tile)
            partial[:, here] = partial[:, here] + summed(table, tiles, ghosts, row, 1, range(nnz - 2 * usual), nnz)

    return rows


def level_rows(level, bounds, rows, total, partial, field, previous, store):
    lower, upper = bounds
    modes, tile = field.shape[0], partial.shape[1] // GROUP
    center = (upper[0] + lower[0]) * 0.5
    factor = 1.0 / jnp.full((modes, tile), (upper[0] - lower[0]) * 0.5, jnp.float32)
    for u, row in enumerate(rows):
        here = columns(row, tile)
        value = total[:, here] + partial[:, u * tile : (u + 1) * tile]
        value = (value - center * field[:, here].astype(jnp.float32)) * factor
        if level == 2:
            value = 2.0 * value - previous[:, here].astype(jnp.float32)
        store(u, row, value.astype(field.dtype))


def next_lists(level, nnz, place, table, order, bounds, tiles, total, near, far, field, previous):
    tile = tiles.shape[1]

    def kernel(place, table, order, lower, upper, tiles, total, near, far, field, *rest):
        if level == 2:
            previous, *rest = rest
        else:
            previous = None
        new_far, new_near, ghosts, partial = rest
        fill_ghosts(place[1], near, far, ghosts)
        for out, first in ((new_far, 0), (new_near, GROUP)):
            rows = ghost_rows(table, order, tiles, ghosts, partial, first, nnz)

            def store(u, row, value, out=out):
                out[:, u * tile : (u + 1) * tile] = value

            level_rows(level, (lower, upper), rows, total, partial, field, previous, store)

    operands = [place, table, order, *bounds, tiles, total, near, far, field] + [previous] * (level == 2)
    return pl.pallas_call(
        kernel,
        out_shape=(shape(far.shape, far.dtype),) * 2,
        in_specs=[SMEM] * 5 + [VMEM] * (len(operands) - 5),
        out_specs=(VMEM,) * 2,
        scratch_shapes=[
            pltpu.VMEM((far.shape[0], 2 * far.shape[1] + tile), far.dtype),
            pltpu.VMEM((far.shape[0], GROUP * tile), jnp.float32),
        ],
        compiler_params=params(8),
        name=f"next_lists_{level}",
    )(*operands)


def next_level(level, nnz, place, table, order, bounds, tiles, total, near, far, field, previous, new_far, new_near):
    modes, width = field.shape
    tile = tiles.shape[1]

    def kernel(place, table, order, lower, upper, tiles, total, near, far, field, new_far, new_near, *rest):
        if level == 2:
            previous, *rest = rest
        else:
            previous = None
        out, ghosts, partial = rest
        fill_ghosts(place[1], near, far, ghosts)
        for held, first in ((new_far, 0), (new_near, GROUP)):
            for u in range(GROUP):
                out[:, columns(order[first + u], tile)] = held[:, u * tile : (u + 1) * tile]

        def store(u, row, value):
            out[:, columns(row, tile)] = value

        def step(i, carry):
            rows = ghost_rows(table, order, tiles, ghosts, partial, i * GROUP, nnz)
            level_rows(level, (lower, upper), rows, total, partial, field, previous, store)
            return carry

        lax.fori_loop(2, order[2 * width // tile], step, 0)

    operands = [place, table, order, *bounds, tiles, total, near, far, field, new_far, new_near]
    operands += [previous] * (level == 2)
    return pl.pallas_call(
        kernel,
        out_shape=shape(field.shape, field.dtype),
        in_specs=[SMEM] * 5 + [VMEM] * (len(operands) - 5),
        out_specs=VMEM,
        scratch_shapes=[
            pltpu.VMEM((modes, 2 * far.shape[1] + tile), far.dtype),
            pltpu.VMEM((modes, GROUP * tile), jnp.float32),
        ],
        compiler_params=params(8),
        cost_estimate=pl.CostEstimate(flops=tiles.size * modes, bytes_accessed=2 * tiles.size, transcendentals=0),
        name=f"next_level_{level}",
    )(*operands)


def last_level(nnz, place, table, send_rows, bounds, tiles, total, near, far, field, previous):
    modes, width = field.shape
    tile = tiles.shape[1]

    def kernel(place, table, send, lower, upper, tiles, total, near, far, field, previous, *rest):
        out, new_far, new_near, ghosts, partial = rest
        core = place[1]
        fill_ghosts(core, near, far, ghosts)

        def store(u, row, value):
            out[:, columns(row, tile)] = value

        def step(i, carry):
            rows = ghost_rows(table, None, tiles, ghosts, partial, i * GROUP, nnz)
            level_rows(2, (lower, upper), rows, total, partial, field, previous, store)
            return carry

        lax.fori_loop(0, width // tile // GROUP, step, 0)
        for slot in range(far.shape[1] // tile):
            here = slice(slot * tile, (slot + 1) * tile)
            new_far[:, here] = out[:, columns(send[core, slot], tile)]
            new_near[:, here] = out[:, columns(send[1 - core, slot], tile)]

    part = shape(far.shape, far.dtype)
    return pl.pallas_call(
        kernel,
        out_shape=(shape(field.shape, field.dtype), part, part),
        in_specs=[SMEM] * 5 + [VMEM] * 6,
        out_specs=(VMEM,) * 3,
        scratch_shapes=[
            pltpu.VMEM((modes, 2 * far.shape[1] + tile), far.dtype),
            pltpu.VMEM((modes, GROUP * tile), jnp.float32),
        ],
        compiler_params=params(8),
        name="last_level",
    )(place, table, send_rows, *bounds, tiles, total, near, far, field, previous)


def partial_sums(nnz, place, table, tiles, total, near, far, own, partner):
    modes, width = own.shape
    tile = tiles.shape[1]
    product = shape((modes, 2 * modes), jnp.float32)

    def kernel(place, table, tiles, total, near, far, own, partner, keep, send, both, ghosts, partial, left):
        mode, core = place[0], place[1]
        fill_ghosts(core, near, far, ghosts)
        both[columns(mode, modes), :] = own[...]
        both[columns(1 - mode, modes), :] = partner[...]
        left[columns(core, modes), :] = own[...]

        def step(i, carry):
            rows = ghost_rows(table, None, tiles, ghosts, partial, i * GROUP, nnz)
            for u, row in enumerate(rows):
                here = columns(row, tile)
                value = total[:, here] + partial[:, u * tile : (u + 1) * tile]
                left[columns(1 - core, modes), here] = value.astype(own.dtype)
            return carry

        lax.fori_loop(0, width // tile // GROUP, step, 0)
        sums = lax.dot_general(left[...], both[...], NT, preferred_element_type=jnp.float32)
        keep[...] = sums[:modes]
        send[...] = sums[modes:]

    return pl.pallas_call(
        kernel,
        out_shape=(product, product, shape((2 * modes, width), own.dtype)),
        in_specs=[SMEM] * 2 + [VMEM] * 6,
        out_specs=(VMEM,) * 3,
        scratch_shapes=[
            pltpu.VMEM((modes, 2 * near.shape[1] + tile), near.dtype),
            pltpu.VMEM((modes, GROUP * tile), jnp.float32),
            pltpu.VMEM((2 * modes, width), own.dtype),
        ],
        compiler_params=params(12),
        name="partial_sums",
    )(place, table, tiles, total, near, far, own, partner)


def sum_over_chips(value):
    for axis in (X, Y, Z):
        others = [flipped(value, axis, bits) for bits in (1, 2, 3)]
        value = (value + others[0]) + (others[1] + others[2])
    return value


def spread(block, lane):
    return jnp.broadcast_to(block[:, lane : lane + 1], block.shape)


def eliminated(blocks):
    rows, size = blocks[0].shape
    sub = lax.broadcasted_iota(jnp.int32, (rows, size), 0)
    lane = lax.broadcasted_iota(jnp.int32, (rows, size), 1)
    blocks = list(blocks)
    for b in range(len(blocks)):
        first = rows * b
        row = [jnp.broadcast_to(blocks[b][s : s + 1, :], (rows, size)) for s in range(rows)]
        d = {(t, s): spread(row[t], first + s) for t in range(rows) for s in range(t + 1)}
        unit = [row[s] + (lane == first + s).astype(jnp.float32) for s in range(rows)]
        ratio, reciprocal = {}, []
        for s in range(rows):
            reciprocal.append(1.0 / d[s, s])
            for t in range(s + 1, rows):
                ratio[t, s] = d[t, s] * reciprocal[s]
            for t in range(s + 1, rows):
                for q in range(s + 1, t + 1):
                    d[t, q] = d[t, q] - ratio[t, s] * d[q, s]
                unit[t] = unit[t] - ratio[t, s] * unit[s]
        solved = [None] * rows
        for s in reversed(range(rows)):
            value = unit[s] * reciprocal[s]
            for t in range(s + 1, rows):
                value = value - ratio[t, s] * solved[t]
            solved[s] = value
        for k in range(b + 1, len(blocks)):
            value = blocks[k]
            for s in range(rows):
                value = value - spread(blocks[k], first + s) * solved[s]
            blocks[k] = value
        value = blocks[b]
        for s in range(rows):
            value = jnp.where(sub == s, unit[s] - (lane == first + s).astype(jnp.float32), value)
        blocks[b] = value
    return blocks


def factor_and_project(place, quarters, both, dof_total):
    modes, width = both.shape[0] // 2, both.shape[1]
    size = 2 * modes

    def kernel(place, own, other_core, other_mode, last, both, basis, ritz, sums, inverse):
        mode, core = place[0], place[1]
        for part, c, m in (
            (own, core, mode),
            (other_core, 1 - core, mode),
            (other_mode, core, 1 - mode),
            (last, 1 - core, 1 - mode),
        ):
            sums[columns(2 * c + m, modes), :] = part[...] / dof_total
        blocks = eliminated([sums[i : i + 8, :] for i in range(0, size, 8)])
        matrix = jnp.concatenate(blocks, axis=0)
        sub = lax.broadcasted_iota(jnp.int32, (size, size), 0)
        lane = lax.broadcasted_iota(jnp.int32, (size, size), 1)
        pivots = jnp.sum(jnp.where(sub == lane, matrix, 0.0), axis=1, keepdims=True)
        lower = jnp.where(lane < sub, matrix, jnp.where(lane == sub, 1.0, 0.0)) * lax.rsqrt(pivots)
        inverse[...] = lower
        left = inverse[columns(mode, modes), :].astype(both.dtype)
        basis[...] = jnp.dot(left, both[...], preferred_element_type=jnp.float32).astype(basis.dtype)
        half = lax.dot_general(
            lower, sums[size:, :], NT, precision=lax.Precision.HIGHEST, preferred_element_type=jnp.float32
        )
        ritz[...] = lax.dot_general(
            half, lower, NT, precision=lax.Precision.HIGHEST, preferred_element_type=jnp.float32
        )

    return pl.pallas_call(
        kernel,
        out_shape=(shape((modes, width), both.dtype), shape((size, size), jnp.float32)),
        in_specs=[SMEM] + [VMEM] * 5,
        out_specs=(VMEM, VMEM),
        scratch_shapes=[pltpu.VMEM((2 * size, size), jnp.float32), pltpu.VMEM((size, size), jnp.float32)],
        compiler_params=params(12),
        name="factor_and_project",
    )(place, *quarters, both)


def shards(stiffness_tiles, tile_cols, send_rows, block, lower_bound, upper_bound):
    rows, nnz, tile, _ = stiffness_tiles.shape
    dof_total = block.shape[0] * lax.axis_size(DOF)
    place = jnp.stack([lax.axis_index(M), lax.axis_index(C)]).astype(jnp.int32)
    bounds = (lower_bound, upper_bound)

    level_0, far, near = pick_lists(place, send_rows, block.T, tile)
    far, near = swapped_between_chips(far), flipped(near, C, 1)
    tiles, total, table, order = stage_and_sum(
        place, send_rows, tile_cols.T, stiffness_tiles.reshape(rows * nnz, tile, tile), level_0
    )

    def exchange(near, far):
        return flipped(near, C, 1), swapped_between_chips(far)

    known = (nnz, place, table, order, bounds, tiles, total, near, far, level_0, None)
    far, near = next_lists(1, *known)
    level_1 = next_level(1, *known, far, near)
    near, far = exchange(near, far)
    total = local_sums(2, table, tiles, level_1, rows, nnz)

    filtered, far, near = last_level(
        nnz, place, table, send_rows, bounds, tiles, total, near, far, level_1, level_0
    )
    partner = flipped(filtered, M, 1)
    near, far = exchange(near, far)
    total = local_sums(3, table, tiles, filtered, rows, nnz)
    keep, send, both = partial_sums(nnz, place, table, tiles, total, near, far, filtered, partner)
    quarter = sum_over_chips(keep + flipped(send, C, 1))
    quarters = (quarter, flipped(quarter, C, 1), flipped(quarter, M, 1), flipped(quarter, (C, M), 3))
    basis, ritz = factor_and_project(place, quarters, both, dof_total)
    return (basis.T, ritz)


def solution(mesh):
    torus = Mesh(mesh.devices.reshape(4, 4, 4, 2, mesh.shape["mode"]), DOF + (M,))
    return jax.shard_map(
        shards,
        mesh=torus,
        in_specs=(P(DOF, None, None, None), P(DOF, None), P(DOF, None), P(DOF, M), P(), P()),
        out_specs=(P(DOF, M), P()),
        check_vma=False,
    )
```

```python
import functools

import jax
import jax.numpy as jnp
from jax import lax
from jax.experimental import pallas as pl
from jax.experimental.pallas import tpu as pltpu
from jax.sharding import Mesh
from jax.sharding import PartitionSpec as P

Z, X, Y, C, M = "dof_z", "dof_x", "dof_y", "dof_c", "mode"
DOF = (Z, X, Y, C)
VMEM = pl.BlockSpec(memory_space=pltpu.VMEM)
SMEM = pl.BlockSpec(memory_space=pltpu.SMEM)
HBM = pl.BlockSpec(memory_space=pltpu.HBM)
NT = (((1,), (1,)), ((), ()))
GROUP = 8
IMAGE_COST = 10**6
IN_FLIGHT = 4


def params(mib):
    return pltpu.CompilerParams(vmem_limit_bytes=mib << 20)


def shape(dims, dtype):
    return jax.ShapeDtypeStruct(dims, dtype)


def flipped(block, axis, bits):
    return lax.ppermute(block, axis, [(i, i ^ bits) for i in range(lax.axis_size(axis))])


def swapped_between_chips(block):
    count = lax.axis_size(DOF)
    pairs = [(i, i + 1) for i in range(1, count - 1, 2)]
    return lax.ppermute(block, DOF, pairs + [(b, a) for a, b in pairs])


def columns(index, tile):
    return pl.ds(pl.multiple_of(index * tile, tile), tile)


def pick_lists(place, send_rows, field, tile):
    modes, width = field.shape
    count = send_rows.shape[1]
    part = shape((modes, count * tile), field.dtype)

    def kernel(place, send, field, held, far, near, rows, sems):
        copies = [
            pltpu.make_async_copy(send, rows, sems.at[0]),
            pltpu.make_async_copy(field, held, sems.at[1]),
        ]
        for copy in copies:
            copy.start()
        for copy in copies:
            copy.wait()
        core = place[1]
        for slot in range(count):
            here = slice(slot * tile, (slot + 1) * tile)
            far[:, here] = held[:, columns(rows[core, slot], tile)]
            near[:, here] = held[:, columns(rows[1 - core, slot], tile)]

    return pl.pallas_call(
        kernel,
        out_shape=(shape(field.shape, field.dtype), part, part),
        in_specs=[SMEM, HBM, HBM],
        out_specs=(VMEM,) * 3,
        scratch_shapes=[pltpu.SMEM(send_rows.shape, jnp.int32), pltpu.SemaphoreType.DMA((2,))],
        compiler_params=params(4),
        name="pick_lists",
    )(
        place,
        pltpu.with_memory_space_constraint(send_rows, pltpu.HBM),
        pltpu.with_memory_space_constraint(field, pltpu.HBM),
    )


def make_plan(core, code, send, table, order, taken):
    nnz, rows, count = len(code), code[0].shape[1], send.shape[1]
    local = [(one < rows).astype(jnp.int32) for one in code]
    locals_before, total = [], jnp.zeros_like(code[0])
    for one in local:
        locals_before.append(total)
        total = total + one
    position = [jnp.where(local[k] == 1, locals_before[k], total + k - locals_before[k]) for k in range(nnz)]
    for p in range(nnz):
        source, entry = jnp.zeros_like(total), jnp.zeros_like(total)
        for k in range(nnz):
            source = jnp.where(position[k] == p, code[k], source)
            entry = jnp.where(position[k] == p, k, entry)
        table[p : p + 1, :] = jnp.where(p < total, source, rows)
        table[nnz + p : nnz + p + 1, :] = jnp.where(p < total, 2 * count, source - rows)
        table[2 * nnz + p : 2 * nnz + p + 1, :] = entry
    table[3 * nnz : 3 * nnz + 1, :] = nnz // 2 - (total >> 1)

    for row in range(rows):
        taken[row] = 0
    for slot in range(count):
        for start, which in ((0, core), (count, 1 - core)):
            row = send[which, slot]
            taken[row] = 1
            order[start + slot] = row
    at = jnp.int32(2 * count)
    for row in range(rows):
        order[at] = row
        at = at + 1 - taken[row]
    for i in range(GROUP):
        order[at + i] = order[0]
    order[2 * rows] = (at + GROUP - 1) // GROUP


def local_row(table, tiles, sources, total, row, nnz):
    total[:, columns(row, tiles.shape[1])] = summed(table, tiles, sources, row, 0, range(nnz - 2), nnz)


def summed(table, tiles, sources, row, kind, positions, nnz):
    tile = tiles.shape[1]
    source = [sources[:, columns(table[kind * nnz + p, row], tile)] for p in positions]
    stored = [tiles[row * nnz + table[2 * nnz + p, row]] for p in positions]
    return jnp.dot(
        jnp.concatenate(source, axis=1), jnp.concatenate(stored, axis=0), preferred_element_type=jnp.float32
    )


def fill_sources(fields, sources):
    at = 0
    for field in fields:
        sources[:, at : at + field.shape[1]] = field[...]
        at += field.shape[1]
    sources[:, at:] = jnp.zeros((sources.shape[0], sources.shape[1] - at), sources.dtype)


def stage_and_sum(place, send_rows, tile_cols, tiles, field):
    modes, width = field.shape
    nnz, rows = tile_cols.shape
    tile = tiles.shape[1]
    per_chunk = GROUP // 2 * nnz
    chunks = rows * nnz // per_chunk
    table_shape = (3 * nnz + 2, rows)

    def kernel(place, send_hbm, cols_hbm, tiles, field, staged, total, table, order, *scratch):
        sources, raw, cols, made, send, taken, sems, small = scratch

        def chunk(i):
            here = pl.ds(i * per_chunk, per_chunk)
            return pltpu.make_async_copy(tiles.at[here], raw.at[here], sems.at[i])

        lists = [
            pltpu.make_async_copy(send_hbm, send, small.at[0]),
            pltpu.make_async_copy(cols_hbm, cols, small.at[1]),
        ]
        for copy in lists:
            copy.start()
        for i in range(IN_FLIGHT):
            chunk(i).start()
        fill_sources((field,), sources)
        def arrive(step):
            for i in (2 * step, 2 * step + 1):
                chunk(i).wait()

                @pl.when(i + IN_FLIGHT < chunks)
                def _():
                    chunk(i + IN_FLIGHT).start()

        def turn(step, u):
            for k in range(nnz):
                at = (step * GROUP + u) * nnz + k
                staged[at] = raw[at].T

        steps = rows // GROUP
        for copy in lists:
            copy.wait()
        arrive(0)
        for u in range(GROUP):
            turn(0, u)
        make_plan(place[1], [cols[k : k + 1, :] for k in range(nnz)], send, made, order, taken)
        copy = pltpu.make_async_copy(made, table, small.at[2])
        copy.start()
        copy.wait()

        def step(i, carry):
            arrive(i + 1)
            for u in range(GROUP):
                turn(i + 1, u)
                local_row(table, staged, sources, total, i * GROUP + u, nnz)
            return carry

        lax.fori_loop(0, steps - 1, step, 0)
        for u in range(GROUP):
            local_row(table, staged, sources, total, (steps - 1) * GROUP + u, nnz)

    def in_hbm(array):
        return pltpu.with_memory_space_constraint(array, pltpu.HBM)

    return pl.pallas_call(
        kernel,
        out_shape=(
            shape(tiles.shape, tiles.dtype),
            shape((modes, width), jnp.float32),
            shape(table_shape, jnp.int32),
            shape((2 * rows + 8,), jnp.int32),
        ),
        in_specs=[SMEM, HBM, HBM, HBM, VMEM],
        out_specs=(VMEM, VMEM, SMEM, SMEM),
        scratch_shapes=[
            pltpu.VMEM((modes, width + tile), field.dtype),
            pltpu.VMEM(tiles.shape, tiles.dtype),
            pltpu.VMEM(tile_cols.shape, jnp.int32),
            pltpu.VMEM(table_shape, jnp.int32),
            pltpu.SMEM(send_rows.shape, jnp.int32),
            pltpu.SMEM((rows,), jnp.int32),
            pltpu.SemaphoreType.DMA((chunks,)),
            pltpu.SemaphoreType.DMA((3,)),
        ],
        compiler_params=params(16),
        cost_estimate=pl.CostEstimate(flops=2 * tiles.size * modes, bytes_accessed=2 * tiles.size, transcendentals=0),
        name="stage_and_sum",
    )(place, in_hbm(send_rows), in_hbm(tile_cols), in_hbm(tiles), field)


def local_sums(level, table, tiles, fields, rows, nnz):
    modes, tile = fields[0].shape[0], tiles.shape[1]
    width = rows * tile

    def kernel(table, tiles, *rest):
        *fields, total, sources = rest
        fill_sources(fields, sources)

        def step(i, carry):
            for u in range(GROUP):
                local_row(table, tiles, sources, total, i * GROUP + u, nnz)
            return carry

        lax.fori_loop(0, rows // GROUP, step, 0)

    return pl.pallas_call(
        kernel,
        out_shape=shape((modes, width), jnp.float32),
        in_specs=[SMEM] + [VMEM] * (1 + len(fields)),
        out_specs=VMEM,
        scratch_shapes=[pltpu.VMEM((modes, width + tile), fields[0].dtype)],
        compiler_params=params(8),
        cost_estimate=pl.CostEstimate(flops=tiles.size * modes // 8, bytes_accessed=0, transcendentals=0),
        name=f"local_sums_{level}",
    )(table, tiles, *fields)


def fill_ghosts(core, near, far, ghosts):
    width = near.shape[1]
    ghosts[:, columns(1 - core, width)] = near[...]
    ghosts[:, columns(core, width)] = far[...]
    ghosts[:, 2 * width :] = jnp.zeros((near.shape[0], ghosts.shape[1] - 2 * width), ghosts.dtype)


def ghost_rows(table, order, tiles, ghosts, partial, first, nnz):
    tile = tiles.shape[1]
    rows = [first + u if order is None else order[first + u] for u in range(GROUP)]
    most = table[3 * nnz, rows[0]]
    for row in rows[1:]:
        most = jnp.maximum(most, table[3 * nnz, row])
    usual = 3
    for u, row in enumerate(rows):
        positions = range(nnz - 2 * usual, nnz)
        partial[:, u * tile : (u + 1) * tile] = summed(table, tiles, ghosts, row, 1, positions, nnz)

    @pl.when(most > usual)
    def _():
        for u, row in enumerate(rows):
            here = slice(u * tile, (u + 1) * tile)
            partial[:, here] = partial[:, here] + summed(table, tiles, ghosts, row, 1, range(nnz - 2 * usual), nnz)

    return rows


def level_rows(level, bounds, rows, total, partial, field, previous, store):
    lower, upper = bounds
    modes, tile = field.shape[0], partial.shape[1] // GROUP
    center = (upper[0] + lower[0]) * 0.5
    factor = 1.0 / jnp.full((modes, tile), (upper[0] - lower[0]) * 0.5, jnp.float32)
    for u, row in enumerate(rows):
        here = columns(row, tile)
        value = total[:, here] + partial[:, u * tile : (u + 1) * tile]
        value = (value - center * field[:, here].astype(jnp.float32)) * factor
        if level == 2:
            value = 2.0 * value - previous[:, here].astype(jnp.float32)
        store(u, row, value.astype(field.dtype))


def next_lists(level, nnz, place, table, order, bounds, tiles, total, near, far, field, previous):
    tile = tiles.shape[1]

    def kernel(place, table, order, lower, upper, tiles, total, near, far, field, *rest):
        if level == 2:
            previous, *rest = rest
        else:
            previous = None
        new_far, new_near, ghosts, partial = rest
        fill_ghosts(place[1], near, far, ghosts)
        for out, first in ((new_far, 0), (new_near, GROUP)):
            rows = ghost_rows(table, order, tiles, ghosts, partial, first, nnz)

            def store(u, row, value, out=out):
                out[:, u * tile : (u + 1) * tile] = value

            level_rows(level, (lower, upper), rows, total, partial, field, previous, store)

    operands = [place, table, order, *bounds, tiles, total, near, far, field] + [previous] * (level == 2)
    return pl.pallas_call(
        kernel,
        out_shape=(shape(far.shape, far.dtype),) * 2,
        in_specs=[SMEM] * 5 + [VMEM] * (len(operands) - 5),
        out_specs=(VMEM,) * 2,
        scratch_shapes=[
            pltpu.VMEM((far.shape[0], 2 * far.shape[1] + tile), far.dtype),
            pltpu.VMEM((far.shape[0], GROUP * tile), jnp.float32),
        ],
        compiler_params=params(8),
        name=f"next_lists_{level}",
    )(*operands)


def next_level(level, nnz, place, table, order, bounds, tiles, total, near, far, field, previous, new_far, new_near):
    modes, width = field.shape
    tile = tiles.shape[1]

    def kernel(place, table, order, lower, upper, tiles, total, near, far, field, new_far, new_near, *rest):
        if level == 2:
            previous, *rest = rest
        else:
            previous = None
        out, ghosts, partial = rest
        fill_ghosts(place[1], near, far, ghosts)
        for held, first in ((new_far, 0), (new_near, GROUP)):
            for u in range(GROUP):
                out[:, columns(order[first + u], tile)] = held[:, u * tile : (u + 1) * tile]

        def store(u, row, value):
            out[:, columns(row, tile)] = value

        def step(i, carry):
            rows = ghost_rows(table, order, tiles, ghosts, partial, i * GROUP, nnz)
            level_rows(level, (lower, upper), rows, total, partial, field, previous, store)
            return carry

        lax.fori_loop(2, order[2 * width // tile], step, 0)

    operands = [place, table, order, *bounds, tiles, total, near, far, field, new_far, new_near]
    operands += [previous] * (level == 2)
    return pl.pallas_call(
        kernel,
        out_shape=shape(field.shape, field.dtype),
        in_specs=[SMEM] * 5 + [VMEM] * (len(operands) - 5),
        out_specs=VMEM,
        scratch_shapes=[
            pltpu.VMEM((modes, 2 * far.shape[1] + tile), far.dtype),
            pltpu.VMEM((modes, GROUP * tile), jnp.float32),
        ],
        compiler_params=params(8),
        cost_estimate=pl.CostEstimate(flops=tiles.size * modes, bytes_accessed=2 * tiles.size, transcendentals=0),
        name=f"next_level_{level}",
    )(*operands)


def last_level(nnz, place, table, send_rows, bounds, tiles, total, near, far, field, previous):
    modes, width = field.shape
    tile = tiles.shape[1]
    groups = width // tile // GROUP

    def kernel(place, table, send, lower, upper, tiles, total, near, far, field, previous, *rest):
        first, second, new_far, new_near, whole, ghosts, partial = rest
        core = place[1]
        fill_ghosts(core, near, far, ghosts)

        def step(i, carry, out, start):
            def store(u, row, value):
                whole[:, columns(row, tile)] = value
                out[:, columns(row - start * GROUP, tile)] = value

            rows = ghost_rows(table, None, tiles, ghosts, partial, i * GROUP, nnz)
            level_rows(2, (lower, upper), rows, total, partial, field, previous, store)
            return carry

        for out, start, stop in ((first, 0, groups - 1), (second, groups - 1, groups)):
            lax.fori_loop(start, stop, functools.partial(step, out=out, start=start), 0)
        for slot in range(far.shape[1] // tile):
            here = slice(slot * tile, (slot + 1) * tile)
            new_far[:, here] = whole[:, columns(send[core, slot], tile)]
            new_near[:, here] = whole[:, columns(send[1 - core, slot], tile)]

    part = shape(far.shape, far.dtype)
    parts = [shape((modes, count * GROUP * tile), field.dtype) for count in (groups - 1, 1)]
    return pl.pallas_call(
        kernel,
        out_shape=(*parts, part, part),
        in_specs=[SMEM] * 5 + [VMEM] * 6,
        out_specs=(VMEM,) * 4,
        scratch_shapes=[
            pltpu.VMEM((modes, width), field.dtype),
            pltpu.VMEM((modes, 2 * far.shape[1] + tile), far.dtype),
            pltpu.VMEM((modes, GROUP * tile), jnp.float32),
        ],
        compiler_params=params(8),
        name="last_level",
    )(place, table, send_rows, *bounds, tiles, total, near, far, field, previous)


def image_rows(nnz, place, table, tiles, total, near, far):
    modes, width = total.shape
    tile = tiles.shape[1]

    def kernel(place, table, tiles, total, near, far, out, ghosts, partial):
        fill_ghosts(place[1], near, far, ghosts)

        def step(i, carry):
            rows = ghost_rows(table, None, tiles, ghosts, partial, i * GROUP, nnz)
            for u, row in enumerate(rows):
                here = columns(row, tile)
                out[:, here] = (total[:, here] + partial[:, u * tile : (u + 1) * tile]).astype(out.dtype)
            return carry

        lax.fori_loop(0, width // tile // GROUP, step, 0)

    return pl.pallas_call(
        kernel,
        out_shape=shape((modes, width), near.dtype),
        in_specs=[SMEM] * 2 + [VMEM] * 4,
        out_specs=VMEM,
        scratch_shapes=[
            pltpu.VMEM((modes, 2 * near.shape[1] + tile), near.dtype),
            pltpu.VMEM((modes, GROUP * tile), jnp.float32),
        ],
        compiler_params=params(8),
        cost_estimate=pl.CostEstimate(flops=IMAGE_COST, bytes_accessed=0, transcendentals=0),
        name="image_rows",
    )(place, table, tiles, total, near, far)


def partial_sums(place, own, partner, image):
    modes, width = image.shape
    product = shape((modes, 2 * modes), jnp.float32)

    def kernel(place, own_first, own_second, first, second, image, keep, send, both, left):
        mode, core = place[0], place[1]
        split = own_first.shape[1]
        for out, row, parts in (
            (both, mode, (own_first, own_second)),
            (both, 1 - mode, (first, second)),
            (left, core, (own_first, own_second)),
        ):
            out[columns(row, modes), :split] = parts[0][...]
            out[columns(row, modes), split:] = parts[1][...]
        left[columns(1 - core, modes), :] = image[...]
        sums = lax.dot_general(left[...], both[...], NT, preferred_element_type=jnp.float32)
        keep[...] = sums[:modes]
        send[...] = sums[modes:]

    return pl.pallas_call(
        kernel,
        out_shape=(product, product, shape((2 * modes, width), image.dtype)),
        in_specs=[SMEM] + [VMEM] * 5,
        out_specs=(VMEM,) * 3,
        scratch_shapes=[pltpu.VMEM((2 * modes, width), image.dtype)],
        compiler_params=params(12),
        name="partial_sums",
    )(place, *own, *partner, image)


def sum_over_chips(value):
    for axis in (X, Y, Z):
        others = [flipped(value, axis, bits) for bits in (1, 2, 3)]
        value = (value + others[0]) + (others[1] + others[2])
    return value


def spread(block, lane):
    return jnp.broadcast_to(block[:, lane : lane + 1], block.shape)


def eliminated(blocks):
    rows, size = blocks[0].shape
    sub = lax.broadcasted_iota(jnp.int32, (rows, size), 0)
    lane = lax.broadcasted_iota(jnp.int32, (rows, size), 1)
    blocks = list(blocks)
    for b in range(len(blocks)):
        first = rows * b
        row = [jnp.broadcast_to(blocks[b][s : s + 1, :], (rows, size)) for s in range(rows)]
        d = {(t, s): spread(row[t], first + s) for t in range(rows) for s in range(t + 1)}
        unit = [row[s] + (lane == first + s).astype(jnp.float32) for s in range(rows)]
        ratio, reciprocal = {}, []
        for s in range(rows):
            reciprocal.append(1.0 / d[s, s])
            for t in range(s + 1, rows):
                ratio[t, s] = d[t, s] * reciprocal[s]
            for t in range(s + 1, rows):
                for q in range(s + 1, t + 1):
                    d[t, q] = d[t, q] - ratio[t, s] * d[q, s]
                unit[t] = unit[t] - ratio[t, s] * unit[s]
        solved = [None] * rows
        for s in reversed(range(rows)):
            value = unit[s] * reciprocal[s]
            for t in range(s + 1, rows):
                value = value - ratio[t, s] * solved[t]
            solved[s] = value
        for k in range(b + 1, len(blocks)):
            value = blocks[k]
            for s in range(rows):
                value = value - spread(blocks[k], first + s) * solved[s]
            blocks[k] = value
        value = blocks[b]
        for s in range(rows):
            value = jnp.where(sub == s, unit[s] - (lane == first + s).astype(jnp.float32), value)
        blocks[b] = value
    return blocks


def factor_and_project(place, quarters, both, dof_total):
    modes, width = both.shape[0] // 2, both.shape[1]
    size = 2 * modes

    def kernel(place, own, other_core, other_mode, last, both, basis, ritz, sums, inverse):
        mode, core = place[0], place[1]
        for part, c, m in (
            (own, core, mode),
            (other_core, 1 - core, mode),
            (other_mode, core, 1 - mode),
            (last, 1 - core, 1 - mode),
        ):
            sums[columns(2 * c + m, modes), :] = part[...] / dof_total
        blocks = eliminated([sums[i : i + 8, :] for i in range(0, size, 8)])
        matrix = jnp.concatenate(blocks, axis=0)
        sub = lax.broadcasted_iota(jnp.int32, (size, size), 0)
        lane = lax.broadcasted_iota(jnp.int32, (size, size), 1)
        pivots = jnp.sum(jnp.where(sub == lane, matrix, 0.0), axis=1, keepdims=True)
        lower = jnp.where(lane < sub, matrix, jnp.where(lane == sub, 1.0, 0.0)) * lax.rsqrt(pivots)
        inverse[...] = lower
        left = inverse[columns(mode, modes), :].astype(both.dtype)
        basis[...] = jnp.dot(left, both[...], preferred_element_type=jnp.float32).astype(basis.dtype)
        half = lax.dot_general(
            lower, sums[size:, :], NT, precision=lax.Precision.HIGHEST, preferred_element_type=jnp.float32
        )
        ritz[...] = lax.dot_general(
            half, lower, NT, precision=lax.Precision.HIGHEST, preferred_element_type=jnp.float32
        )

    return pl.pallas_call(
        kernel,
        out_shape=(shape((modes, width), both.dtype), shape((size, size), jnp.float32)),
        in_specs=[SMEM] + [VMEM] * 5,
        out_specs=(VMEM, VMEM),
        scratch_shapes=[pltpu.VMEM((2 * size, size), jnp.float32), pltpu.VMEM((size, size), jnp.float32)],
        compiler_params=params(12),
        name="factor_and_project",
    )(place, *quarters, both)


def shards(stiffness_tiles, tile_cols, send_rows, block, lower_bound, upper_bound):
    rows, nnz, tile, _ = stiffness_tiles.shape
    dof_total = block.shape[0] * lax.axis_size(DOF)
    place = jnp.stack([lax.axis_index(M), lax.axis_index(C)]).astype(jnp.int32)
    bounds = (lower_bound, upper_bound)

    level_0, far, near = pick_lists(place, send_rows, block.T, tile)
    far, near = swapped_between_chips(far), flipped(near, C, 1)
    tiles, total, table, order = stage_and_sum(
        place, send_rows, tile_cols.T, stiffness_tiles.reshape(rows * nnz, tile, tile), level_0
    )

    def exchange(near, far):
        return flipped(near, C, 1), swapped_between_chips(far)

    known = (nnz, place, table, order, bounds, tiles, total, near, far, level_0, None)
    far, near = next_lists(1, *known)
    level_1 = next_level(1, *known, far, near)
    near, far = exchange(near, far)
    total = local_sums(2, table, tiles, (level_1,), rows, nnz)

    *filtered, far, near = last_level(
        nnz, place, table, send_rows, bounds, tiles, total, near, far, level_1, level_0
    )
    near, far = exchange(near, far)
    partner = [flipped(part, M, 1) for part in filtered]
    total = local_sums(3, table, tiles, filtered, rows, nnz)
    image = image_rows(nnz, place, table, tiles, total, near, far)
    keep, send, both = partial_sums(place, filtered, partner, image)
    quarter = sum_over_chips(keep + flipped(send, C, 1))
    quarters = (quarter, flipped(quarter, C, 1), flipped(quarter, M, 1), flipped(quarter, (C, M), 3))
    basis, ritz = factor_and_project(place, quarters, both, dof_total)
    return (basis.T, ritz)


def solution(mesh):
    torus = Mesh(mesh.devices.reshape(4, 4, 4, 2, mesh.shape["mode"]), DOF + (M,))
    return jax.shard_map(
        shards,
        mesh=torus,
        in_specs=(P(DOF, None, None, None), P(DOF, None), P(DOF, None), P(DOF, M), P(), P()),
        out_specs=(P(DOF, M), P()),
        check_vma=False,
    )
```

```python
import functools

import jax
import jax.numpy as jnp
from jax import lax
from jax.experimental import pallas as pl
from jax.experimental.pallas import tpu as pltpu
from jax.sharding import Mesh
from jax.sharding import PartitionSpec as P

Z, X, Y, C, M = "dof_z", "dof_x", "dof_y", "dof_c", "mode"
DOF = (Z, X, Y, C)
VMEM = pl.BlockSpec(memory_space=pltpu.VMEM)
SMEM = pl.BlockSpec(memory_space=pltpu.SMEM)
HBM = pl.BlockSpec(memory_space=pltpu.HBM)
NT = (((1,), (1,)), ((), ()))
GROUP = 8
IMAGE_COST = 10**6
IN_FLIGHT = 4


def params(mib):
    return pltpu.CompilerParams(vmem_limit_bytes=mib << 20)


def shape(dims, dtype):
    return jax.ShapeDtypeStruct(dims, dtype)


def flipped(block, axis, bits):
    return lax.ppermute(block, axis, [(i, i ^ bits) for i in range(lax.axis_size(axis))])


def swapped_between_chips(block):
    count = lax.axis_size(DOF)
    pairs = [(i, i + 1) for i in range(1, count - 1, 2)]
    return lax.ppermute(block, DOF, pairs + [(b, a) for a, b in pairs])


def columns(index, tile):
    return pl.ds(pl.multiple_of(index * tile, tile), tile)


def pick_lists(place, send_rows, field, tile):
    modes, width = field.shape
    count = send_rows.shape[1]
    part = shape((modes, count * tile), field.dtype)

    def kernel(place, send, field, held, far, near, rows, sems):
        copies = [
            pltpu.make_async_copy(send, rows, sems.at[0]),
            pltpu.make_async_copy(field, held, sems.at[1]),
        ]
        for copy in copies:
            copy.start()
        for copy in copies:
            copy.wait()
        core = place[1]
        for slot in range(count):
            here = slice(slot * tile, (slot + 1) * tile)
            far[:, here] = held[:, columns(rows[core, slot], tile)]
            near[:, here] = held[:, columns(rows[1 - core, slot], tile)]

    return pl.pallas_call(
        kernel,
        out_shape=(shape(field.shape, field.dtype), part, part),
        in_specs=[SMEM, HBM, HBM],
        out_specs=(VMEM,) * 3,
        scratch_shapes=[pltpu.SMEM(send_rows.shape, jnp.int32), pltpu.SemaphoreType.DMA((2,))],
        compiler_params=params(4),
        name="pick_lists",
    )(
        place,
        pltpu.with_memory_space_constraint(send_rows, pltpu.HBM),
        pltpu.with_memory_space_constraint(field, pltpu.HBM),
    )


def make_plan(core, code, send, table, order, taken):
    nnz, rows, count = len(code), code[0].shape[1], send.shape[1]
    local = [(one < rows).astype(jnp.int32) for one in code]
    locals_before, total = [], jnp.zeros_like(code[0])
    for one in local:
        locals_before.append(total)
        total = total + one
    position = [jnp.where(local[k] == 1, locals_before[k], total + k - locals_before[k]) for k in range(nnz)]
    for p in range(nnz):
        source, entry = jnp.zeros_like(total), jnp.zeros_like(total)
        for k in range(nnz):
            source = jnp.where(position[k] == p, code[k], source)
            entry = jnp.where(position[k] == p, k, entry)
        table[p : p + 1, :] = jnp.where(p < total, source, rows)
        table[nnz + p : nnz + p + 1, :] = jnp.where(p < total, 2 * count, source - rows)
        table[2 * nnz + p : 2 * nnz + p + 1, :] = entry
    table[3 * nnz : 3 * nnz + 1, :] = nnz // 2 - (total >> 1)

    for row in range(rows):
        taken[row] = 0
    for slot in range(count):
        for start, which in ((0, core), (count, 1 - core)):
            row = send[which, slot]
            taken[row] = 1
            order[start + slot] = row
    at = jnp.int32(2 * count)
    for row in range(rows):
        order[at] = row
        at = at + 1 - taken[row]
    for i in range(GROUP):
        order[at + i] = order[0]
    order[2 * rows] = (at + GROUP - 1) // GROUP


def local_row(table, tiles, sources, total, row, nnz):
    total[:, columns(row, tiles.shape[1])] = summed(table, tiles, sources, row, 0, range(nnz - 2), nnz)


def summed(table, tiles, sources, row, kind, positions, nnz):
    tile = tiles.shape[1]
    source = [sources[:, columns(table[kind * nnz + p, row], tile)] for p in positions]
    stored = [tiles[row * nnz + table[2 * nnz + p, row]] for p in positions]
    return jnp.dot(
        jnp.concatenate(source, axis=1), jnp.concatenate(stored, axis=0), preferred_element_type=jnp.float32
    )


def fill_sources(fields, sources):
    at = 0
    for field in fields:
        sources[:, at : at + field.shape[1]] = field[...]
        at += field.shape[1]
    sources[:, at:] = jnp.zeros((sources.shape[0], sources.shape[1] - at), sources.dtype)


def stage_and_sum(place, send_rows, tile_cols, tiles, field):
    modes, width = field.shape
    nnz, rows = tile_cols.shape
    tile = tiles.shape[1]
    per_chunk = GROUP // 2 * nnz
    chunks = rows * nnz // per_chunk
    table_shape = (3 * nnz + 2, rows)

    def kernel(place, send_hbm, cols_hbm, tiles, field, staged, total, table, order, *scratch):
        sources, raw, cols, made, send, taken, sems, small = scratch

        def chunk(i):
            here = pl.ds(i * per_chunk, per_chunk)
            return pltpu.make_async_copy(tiles.at[here], raw.at[here], sems.at[i])

        lists = [
            pltpu.make_async_copy(send_hbm, send, small.at[0]),
            pltpu.make_async_copy(cols_hbm, cols, small.at[1]),
        ]
        for copy in lists:
            copy.start()
        for i in range(IN_FLIGHT):
            chunk(i).start()
        fill_sources((field,), sources)
        def arrive(step):
            for i in (2 * step, 2 * step + 1):
                chunk(i).wait()

                @pl.when(i + IN_FLIGHT < chunks)
                def _():
                    chunk(i + IN_FLIGHT).start()

        def turn(step, u):
            for k in range(nnz):
                at = (step * GROUP + u) * nnz + k
                staged[at] = raw[at].T

        steps = rows // GROUP
        for copy in lists:
            copy.wait()
        arrive(0)
        for u in range(GROUP):
            turn(0, u)
        make_plan(place[1], [cols[k : k + 1, :] for k in range(nnz)], send, made, order, taken)
        copy = pltpu.make_async_copy(made, table, small.at[2])
        copy.start()
        copy.wait()

        def step(i, carry):
            arrive(i + 1)
            for u in range(GROUP):
                turn(i + 1, u)
                local_row(table, staged, sources, total, i * GROUP + u, nnz)
            return carry

        lax.fori_loop(0, steps - 1, step, 0)
        for u in range(GROUP):
            local_row(table, staged, sources, total, (steps - 1) * GROUP + u, nnz)

    def in_hbm(array):
        return pltpu.with_memory_space_constraint(array, pltpu.HBM)

    return pl.pallas_call(
        kernel,
        out_shape=(
            shape(tiles.shape, tiles.dtype),
            shape((modes, width), jnp.float32),
            shape(table_shape, jnp.int32),
            shape((2 * rows + 8,), jnp.int32),
        ),
        in_specs=[SMEM, HBM, HBM, HBM, VMEM],
        out_specs=(VMEM, VMEM, SMEM, SMEM),
        scratch_shapes=[
            pltpu.VMEM((modes, width + tile), field.dtype),
            pltpu.VMEM(tiles.shape, tiles.dtype),
            pltpu.VMEM(tile_cols.shape, jnp.int32),
            pltpu.VMEM(table_shape, jnp.int32),
            pltpu.SMEM(send_rows.shape, jnp.int32),
            pltpu.SMEM((rows,), jnp.int32),
            pltpu.SemaphoreType.DMA((chunks,)),
            pltpu.SemaphoreType.DMA((3,)),
        ],
        compiler_params=params(16),
        cost_estimate=pl.CostEstimate(flops=2 * tiles.size * modes, bytes_accessed=2 * tiles.size, transcendentals=0),
        name="stage_and_sum",
    )(place, in_hbm(send_rows), in_hbm(tile_cols), in_hbm(tiles), field)


def local_sums(level, table, tiles, fields, rows, nnz):
    modes, tile = fields[0].shape[0], tiles.shape[1]
    width = rows * tile

    def kernel(table, tiles, *rest):
        *fields, total, sources = rest
        fill_sources(fields, sources)

        def step(i, carry):
            for u in range(GROUP):
                local_row(table, tiles, sources, total, i * GROUP + u, nnz)
            return carry

        lax.fori_loop(0, rows // GROUP, step, 0)

    return pl.pallas_call(
        kernel,
        out_shape=shape((modes, width), jnp.float32),
        in_specs=[SMEM] + [VMEM] * (1 + len(fields)),
        out_specs=VMEM,
        scratch_shapes=[pltpu.VMEM((modes, width + tile), fields[0].dtype)],
        compiler_params=params(8),
        cost_estimate=pl.CostEstimate(flops=tiles.size * modes // 8, bytes_accessed=0, transcendentals=0),
        name=f"local_sums_{level}",
    )(table, tiles, *fields)


def fill_ghosts(core, near, far, ghosts):
    width = near.shape[1]
    ghosts[:, columns(1 - core, width)] = near[...]
    ghosts[:, columns(core, width)] = far[...]
    ghosts[:, 2 * width :] = jnp.zeros((near.shape[0], ghosts.shape[1] - 2 * width), ghosts.dtype)


def ghost_rows(table, order, tiles, ghosts, partial, first, nnz):
    tile = tiles.shape[1]
    rows = [first + u if order is None else order[first + u] for u in range(GROUP)]
    most = table[3 * nnz, rows[0]]
    for row in rows[1:]:
        most = jnp.maximum(most, table[3 * nnz, row])
    usual = 3
    for u, row in enumerate(rows):
        positions = range(nnz - 2 * usual, nnz)
        partial[:, u * tile : (u + 1) * tile] = summed(table, tiles, ghosts, row, 1, positions, nnz)

    @pl.when(most > usual)
    def _():
        for u, row in enumerate(rows):
            here = slice(u * tile, (u + 1) * tile)
            partial[:, here] = partial[:, here] + summed(table, tiles, ghosts, row, 1, range(nnz - 2 * usual), nnz)

    return rows


def level_rows(level, bounds, rows, total, partial, field, previous, store):
    lower, upper = bounds
    modes, tile = field.shape[0], partial.shape[1] // GROUP
    center = (upper[0] + lower[0]) * 0.5
    factor = 1.0 / jnp.full((modes, tile), (upper[0] - lower[0]) * 0.5, jnp.float32)
    for u, row in enumerate(rows):
        here = columns(row, tile)
        value = total[:, here] + partial[:, u * tile : (u + 1) * tile]
        value = (value - center * field[:, here].astype(jnp.float32)) * factor
        if level == 2:
            value = 2.0 * value - previous[:, here].astype(jnp.float32)
        store(u, row, value.astype(field.dtype))


def next_lists(level, nnz, place, table, order, bounds, tiles, total, near, far, field, previous):
    tile = tiles.shape[1]

    def kernel(place, table, order, lower, upper, tiles, total, near, far, field, *rest):
        if level == 2:
            previous, *rest = rest
        else:
            previous = None
        new_far, new_near, ghosts, partial = rest
        fill_ghosts(place[1], near, far, ghosts)
        for out, first in ((new_far, 0), (new_near, GROUP)):
            rows = ghost_rows(table, order, tiles, ghosts, partial, first, nnz)

            def store(u, row, value, out=out):
                out[:, u * tile : (u + 1) * tile] = value

            level_rows(level, (lower, upper), rows, total, partial, field, previous, store)

    operands = [place, table, order, *bounds, tiles, total, near, far, field] + [previous] * (level == 2)
    return pl.pallas_call(
        kernel,
        out_shape=(shape(far.shape, far.dtype),) * 2,
        in_specs=[SMEM] * 5 + [VMEM] * (len(operands) - 5),
        out_specs=(VMEM,) * 2,
        scratch_shapes=[
            pltpu.VMEM((far.shape[0], 2 * far.shape[1] + tile), far.dtype),
            pltpu.VMEM((far.shape[0], GROUP * tile), jnp.float32),
        ],
        compiler_params=params(8),
        name=f"next_lists_{level}",
    )(*operands)


def next_level(level, nnz, place, table, order, bounds, tiles, total, near, far, field, previous, new_far, new_near):
    modes, width = field.shape
    tile = tiles.shape[1]

    def kernel(place, table, order, lower, upper, tiles, total, near, far, field, new_far, new_near, *rest):
        if level == 2:
            previous, *rest = rest
        else:
            previous = None
        out, ghosts, partial = rest
        fill_ghosts(place[1], near, far, ghosts)
        for held, first in ((new_far, 0), (new_near, GROUP)):
            for u in range(GROUP):
                out[:, columns(order[first + u], tile)] = held[:, u * tile : (u + 1) * tile]

        def store(u, row, value):
            out[:, columns(row, tile)] = value

        def step(i, carry):
            rows = ghost_rows(table, order, tiles, ghosts, partial, i * GROUP, nnz)
            level_rows(level, (lower, upper), rows, total, partial, field, previous, store)
            return carry

        lax.fori_loop(2, order[2 * width // tile], step, 0)

    operands = [place, table, order, *bounds, tiles, total, near, far, field, new_far, new_near]
    operands += [previous] * (level == 2)
    return pl.pallas_call(
        kernel,
        out_shape=shape(field.shape, field.dtype),
        in_specs=[SMEM] * 5 + [VMEM] * (len(operands) - 5),
        out_specs=VMEM,
        scratch_shapes=[
            pltpu.VMEM((modes, 2 * far.shape[1] + tile), far.dtype),
            pltpu.VMEM((modes, GROUP * tile), jnp.float32),
        ],
        compiler_params=params(8),
        cost_estimate=pl.CostEstimate(flops=tiles.size * modes, bytes_accessed=2 * tiles.size, transcendentals=0),
        name=f"next_level_{level}",
    )(*operands)


def last_level(nnz, place, table, send_rows, bounds, tiles, total, near, far, field, previous):
    modes, width = field.shape
    tile = tiles.shape[1]
    groups = width // tile // GROUP

    def kernel(place, table, send, lower, upper, tiles, total, near, far, field, previous, *rest):
        first, second, new_far, new_near, whole, ghosts, partial = rest
        core = place[1]
        fill_ghosts(core, near, far, ghosts)

        def step(i, carry, out, start):
            def store(u, row, value):
                whole[:, columns(row, tile)] = value
                out[:, columns(row - start * GROUP, tile)] = value

            rows = ghost_rows(table, None, tiles, ghosts, partial, i * GROUP, nnz)
            level_rows(2, (lower, upper), rows, total, partial, field, previous, store)
            return carry

        for out, start, stop in ((first, 0, groups - 1), (second, groups - 1, groups)):
            lax.fori_loop(start, stop, functools.partial(step, out=out, start=start), 0)
        for slot in range(far.shape[1] // tile):
            here = slice(slot * tile, (slot + 1) * tile)
            new_far[:, here] = whole[:, columns(send[core, slot], tile)]
            new_near[:, here] = whole[:, columns(send[1 - core, slot], tile)]

    part = shape(far.shape, far.dtype)
    parts = [shape((modes, count * GROUP * tile), field.dtype) for count in (groups - 1, 1)]
    return pl.pallas_call(
        kernel,
        out_shape=(*parts, part, part),
        in_specs=[SMEM] * 5 + [VMEM] * 6,
        out_specs=(VMEM,) * 4,
        scratch_shapes=[
            pltpu.VMEM((modes, width), field.dtype),
            pltpu.VMEM((modes, 2 * far.shape[1] + tile), far.dtype),
            pltpu.VMEM((modes, GROUP * tile), jnp.float32),
        ],
        compiler_params=params(8),
        name="last_level",
    )(place, table, send_rows, *bounds, tiles, total, near, far, field, previous)


def image_rows(nnz, place, table, tiles, total, near, far):
    modes, width = total.shape
    tile = tiles.shape[1]

    def kernel(place, table, tiles, total, near, far, out, ghosts, partial):
        fill_ghosts(place[1], near, far, ghosts)

        def step(i, carry):
            rows = ghost_rows(table, None, tiles, ghosts, partial, i * GROUP, nnz)
            for u, row in enumerate(rows):
                here = columns(row, tile)
                out[:, here] = (total[:, here] + partial[:, u * tile : (u + 1) * tile]).astype(out.dtype)
            return carry

        lax.fori_loop(0, width // tile // GROUP, step, 0)

    return pl.pallas_call(
        kernel,
        out_shape=shape((modes, width), near.dtype),
        in_specs=[SMEM] * 2 + [VMEM] * 4,
        out_specs=VMEM,
        scratch_shapes=[
            pltpu.VMEM((modes, 2 * near.shape[1] + tile), near.dtype),
            pltpu.VMEM((modes, GROUP * tile), jnp.float32),
        ],
        compiler_params=params(8),
        cost_estimate=pl.CostEstimate(flops=IMAGE_COST, bytes_accessed=0, transcendentals=0),
        name="image_rows",
    )(place, table, tiles, total, near, far)


def partial_sums(place, own, partner, image):
    modes, width = image.shape
    product = shape((modes, 2 * modes), jnp.float32)

    def kernel(place, own_first, own_second, first, second, image, keep, send, both, left):
        mode, core = place[0], place[1]
        split = own_first.shape[1]
        for out, row, parts in (
            (both, mode, (own_first, own_second)),
            (both, 1 - mode, (first, second)),
            (left, core, (own_first, own_second)),
        ):
            out[columns(row, modes), :split] = parts[0][...]
            out[columns(row, modes), split:] = parts[1][...]
        left[columns(1 - core, modes), :] = image[...]
        sums = lax.dot_general(left[...], both[...], NT, preferred_element_type=jnp.float32)
        keep[...] = sums[:modes]
        send[...] = sums[modes:]

    return pl.pallas_call(
        kernel,
        out_shape=(product, product, shape((2 * modes, width), image.dtype)),
        in_specs=[SMEM] + [VMEM] * 5,
        out_specs=(VMEM,) * 3,
        scratch_shapes=[pltpu.VMEM((2 * modes, width), image.dtype)],
        compiler_params=params(12),
        name="partial_sums",
    )(place, *own, *partner, image)


def sum_over_chips(value):
    for axis in (X, Y, Z):
        others = [flipped(value, axis, bits) for bits in (1, 3, 2)]
        value = (value + others[0]) + (others[1] + others[2])
    return value


def spread(block, lane):
    return jnp.broadcast_to(block[:, lane : lane + 1], block.shape)


def eliminated(blocks):
    rows, size = blocks[0].shape
    sub = lax.broadcasted_iota(jnp.int32, (rows, size), 0)
    lane = lax.broadcasted_iota(jnp.int32, (rows, size), 1)
    blocks = list(blocks)
    for b in range(len(blocks)):
        first = rows * b
        row = [jnp.broadcast_to(blocks[b][s : s + 1, :], (rows, size)) for s in range(rows)]
        d = {(t, s): spread(row[t], first + s) for t in range(rows) for s in range(t + 1)}
        unit = [row[s] + (lane == first + s).astype(jnp.float32) for s in range(rows)]
        ratio, reciprocal = {}, []
        for s in range(rows):
            reciprocal.append(1.0 / d[s, s])
            for t in range(s + 1, rows):
                ratio[t, s] = d[t, s] * reciprocal[s]
            for t in range(s + 1, rows):
                for q in range(s + 1, t + 1):
                    d[t, q] = d[t, q] - ratio[t, s] * d[q, s]
                unit[t] = unit[t] - ratio[t, s] * unit[s]
        solved = [None] * rows
        for s in reversed(range(rows)):
            value = unit[s] * reciprocal[s]
            for t in reversed(range(s + 1, rows)):
                value = value - ratio[t, s] * solved[t]
            solved[s] = value
        for k in range(b + 1, len(blocks)):
            value = blocks[k]
            for s in reversed(range(rows)):
                value = value - spread(blocks[k], first + s) * solved[s]
            blocks[k] = value
        value = blocks[b]
        for s in range(rows):
            value = jnp.where(sub == s, unit[s] - (lane == first + s).astype(jnp.float32), value)
        blocks[b] = value
    return blocks


def factor_and_project(place, quarters, both, dof_total):
    modes, width = both.shape[0] // 2, both.shape[1]
    size = 2 * modes

    def kernel(place, own, other_core, other_mode, last, both, basis, ritz, sums, inverse):
        mode, core = place[0], place[1]
        for part, c, m in (
            (own, core, mode),
            (other_core, 1 - core, mode),
            (other_mode, core, 1 - mode),
            (last, 1 - core, 1 - mode),
        ):
            sums[columns(2 * c + m, modes), :] = part[...] / dof_total
        blocks = eliminated([sums[i : i + 8, :] for i in range(0, size, 8)])
        matrix = jnp.concatenate(blocks, axis=0)
        sub = lax.broadcasted_iota(jnp.int32, (size, size), 0)
        lane = lax.broadcasted_iota(jnp.int32, (size, size), 1)
        pivots = jnp.sum(jnp.where(sub == lane, matrix, 0.0), axis=1, keepdims=True)
        lower = jnp.where(lane < sub, matrix, jnp.where(lane == sub, 1.0, 0.0)) * lax.rsqrt(pivots)
        inverse[...] = lower
        left = inverse[columns(mode, modes), :].astype(both.dtype)
        basis[...] = jnp.dot(left, both[...], preferred_element_type=jnp.float32).astype(basis.dtype)
        half = lax.dot_general(
            lower, sums[size:, :], NT, precision=lax.Precision.HIGHEST, preferred_element_type=jnp.float32
        )
        ritz[...] = lax.dot_general(
            half, lower, NT, precision=lax.Precision.HIGHEST, preferred_element_type=jnp.float32
        )

    return pl.pallas_call(
        kernel,
        out_shape=(shape((modes, width), both.dtype), shape((size, size), jnp.float32)),
        in_specs=[SMEM] + [VMEM] * 5,
        out_specs=(VMEM, VMEM),
        scratch_shapes=[pltpu.VMEM((2 * size, size), jnp.float32), pltpu.VMEM((size, size), jnp.float32)],
        compiler_params=params(12),
        name="factor_and_project",
    )(place, *quarters, both)


def shards(stiffness_tiles, tile_cols, send_rows, block, lower_bound, upper_bound):
    rows, nnz, tile, _ = stiffness_tiles.shape
    dof_total = block.shape[0] * lax.axis_size(DOF)
    place = jnp.stack([lax.axis_index(M), lax.axis_index(C)]).astype(jnp.int32)
    bounds = (lower_bound, upper_bound)

    level_0, far, near = pick_lists(place, send_rows, block.T, tile)
    far, near = swapped_between_chips(far), flipped(near, C, 1)
    tiles, total, table, order = stage_and_sum(
        place, send_rows, tile_cols.T, stiffness_tiles.reshape(rows * nnz, tile, tile), level_0
    )

    def exchange(near, far):
        return flipped(near, C, 1), swapped_between_chips(far)

    known = (nnz, place, table, order, bounds, tiles, total, near, far, level_0, None)
    far, near = next_lists(1, *known)
    level_1 = next_level(1, *known, far, near)
    near, far = exchange(near, far)
    total = local_sums(2, table, tiles, (level_1,), rows, nnz)

    *filtered, far, near = last_level(
        nnz, place, table, send_rows, bounds, tiles, total, near, far, level_1, level_0
    )
    near, far = exchange(near, far)
    partner = [flipped(part, M, 1) for part in filtered]
    total = local_sums(3, table, tiles, filtered, rows, nnz)
    image = image_rows(nnz, place, table, tiles, total, near, far)
    keep, send, both = partial_sums(place, filtered, partner, image)
    quarter = sum_over_chips(keep + flipped(send, C, 1))
    quarters = (quarter, flipped(quarter, C, 1), flipped(quarter, M, 1), flipped(quarter, (C, M), 3))
    basis, ritz = factor_and_project(place, quarters, both, dof_total)
    return (basis.T, ritz)


def solution(mesh):
    torus = Mesh(mesh.devices.reshape(4, 4, 4, 2, mesh.shape["mode"]), DOF + (M,))
    return jax.shard_map(
        shards,
        mesh=torus,
        in_specs=(P(DOF, None, None, None), P(DOF, None), P(DOF, None), P(DOF, M), P(), P()),
        out_specs=(P(DOF, M), P()),
        check_vma=False,
    )
```

```python
import jax
import jax.numpy as jnp
from jax import lax
from jax.experimental import pallas as pl
from jax.experimental.pallas import tpu as pltpu
from jax.sharding import Mesh
from jax.sharding import PartitionSpec as P

Z, X, Y, C, M = "dof_z", "dof_x", "dof_y", "dof_c", "mode"
DOF = (Z, X, Y, C)
VMEM = pl.BlockSpec(memory_space=pltpu.VMEM)
SMEM = pl.BlockSpec(memory_space=pltpu.SMEM)
HBM = pl.BlockSpec(memory_space=pltpu.HBM)
NT = (((1,), (1,)), ((), ()))
GROUP = 8
IMAGE_COST = 10**9
FIRST_PART = 20
IN_FLIGHT = 4


def params(mib):
    return pltpu.CompilerParams(vmem_limit_bytes=mib << 20)


def shape(dims, dtype):
    return jax.ShapeDtypeStruct(dims, dtype)


def flipped(block, axis, bits):
    return lax.ppermute(block, axis, [(i, i ^ bits) for i in range(lax.axis_size(axis))])


def swapped_between_chips(block):
    count = lax.axis_size(DOF)
    pairs = [(i, i + 1) for i in range(1, count - 1, 2)]
    return lax.ppermute(block, DOF, pairs + [(b, a) for a, b in pairs])


def columns(index, tile):
    return pl.ds(pl.multiple_of(index * tile, tile), tile)


def pick_lists(place, send_rows, field, tile):
    modes, width = field.shape
    count = send_rows.shape[1]
    part = shape((modes, count * tile), field.dtype)

    def kernel(place, send, field, held, far, near, rows, sems):
        copies = [
            pltpu.make_async_copy(send, rows, sems.at[0]),
            pltpu.make_async_copy(field, held, sems.at[1]),
        ]
        for copy in copies:
            copy.start()
        for copy in copies:
            copy.wait()
        core = place[1]
        for slot in range(count):
            here = slice(slot * tile, (slot + 1) * tile)
            far[:, here] = held[:, columns(rows[core, slot], tile)]
            near[:, here] = held[:, columns(rows[1 - core, slot], tile)]

    return pl.pallas_call(
        kernel,
        out_shape=(shape(field.shape, field.dtype), part, part),
        in_specs=[SMEM, HBM, HBM],
        out_specs=(VMEM,) * 3,
        scratch_shapes=[pltpu.SMEM(send_rows.shape, jnp.int32), pltpu.SemaphoreType.DMA((2,))],
        compiler_params=params(4),
        name="pick_lists",
    )(
        place,
        pltpu.with_memory_space_constraint(send_rows, pltpu.HBM),
        pltpu.with_memory_space_constraint(field, pltpu.HBM),
    )


def make_plan(core, code, send, table, order, taken):
    nnz, rows, count = len(code), code[0].shape[1], send.shape[1]
    local = [(one < rows).astype(jnp.int32) for one in code]
    locals_before, total = [], jnp.zeros_like(code[0])
    for one in local:
        locals_before.append(total)
        total = total + one
    position = [jnp.where(local[k] == 1, locals_before[k], total + k - locals_before[k]) for k in range(nnz)]
    for p in range(nnz):
        source, entry = jnp.zeros_like(total), jnp.zeros_like(total)
        for k in range(nnz):
            source = jnp.where(position[k] == p, code[k], source)
            entry = jnp.where(position[k] == p, k, entry)
        table[p : p + 1, :] = jnp.where(p < total, source, rows)
        table[nnz + p : nnz + p + 1, :] = jnp.where(p < total, 2 * count, source - rows)
        table[2 * nnz + p : 2 * nnz + p + 1, :] = entry
    table[3 * nnz : 3 * nnz + 1, :] = nnz // 2 - (total >> 1)

    for row in range(rows):
        taken[row] = 0
    for slot in range(count):
        for start, which in ((0, core), (count, 1 - core)):
            row = send[which, slot]
            taken[row] = 1
            order[start + slot] = row
    at = jnp.int32(2 * count)
    for row in range(rows):
        order[at] = row
        at = at + 1 - taken[row]
    for i in range(GROUP):
        order[at + i] = order[0]
    order[2 * rows] = (at + GROUP - 1) // GROUP


def local_row(table, tiles, sources, total, row, nnz):
    total[:, columns(row, tiles.shape[1])] = summed(table, tiles, sources, row, 0, range(nnz - 2), nnz)


def summed(table, tiles, sources, row, kind, positions, nnz):
    tile = tiles.shape[1]
    source = [sources[:, columns(table[kind * nnz + p, row], tile)] for p in positions]
    stored = [tiles[row * nnz + table[2 * nnz + p, row]] for p in positions]
    return jnp.dot(
        jnp.concatenate(source, axis=1), jnp.concatenate(stored, axis=0), preferred_element_type=jnp.float32
    )


def fill_sources(fields, sources):
    at = 0
    for field in fields:
        sources[:, at : at + field.shape[1]] = field[...]
        at += field.shape[1]
    sources[:, at:] = jnp.zeros((sources.shape[0], sources.shape[1] - at), sources.dtype)


def stage_and_sum(place, send_rows, tile_cols, tiles, field):
    modes, width = field.shape
    nnz, rows = tile_cols.shape
    tile = tiles.shape[1]
    per_chunk = GROUP // 2 * nnz
    chunks = rows * nnz // per_chunk
    table_shape = (3 * nnz + 2, rows)

    def kernel(place, send_hbm, cols_hbm, tiles, field, staged, total, table, order, *scratch):
        sources, raw, cols, made, send, taken, sems, small = scratch

        def chunk(i):
            here = pl.ds(i * per_chunk, per_chunk)
            return pltpu.make_async_copy(tiles.at[here], raw.at[here], sems.at[i])

        lists = [
            pltpu.make_async_copy(send_hbm, send, small.at[0]),
            pltpu.make_async_copy(cols_hbm, cols, small.at[1]),
        ]
        for copy in lists:
            copy.start()
        for i in range(IN_FLIGHT):
            chunk(i).start()
        fill_sources((field,), sources)
        def arrive(step):
            for i in (2 * step, 2 * step + 1):
                chunk(i).wait()

                @pl.when(i + IN_FLIGHT < chunks)
                def _():
                    chunk(i + IN_FLIGHT).start()

        def turn(step, u):
            for k in range(nnz):
                at = (step * GROUP + u) * nnz + k
                staged[at] = raw[at].T

        steps = rows // GROUP
        for copy in lists:
            copy.wait()
        arrive(0)
        for u in range(GROUP):
            turn(0, u)
        make_plan(place[1], [cols[k : k + 1, :] for k in range(nnz)], send, made, order, taken)
        copy = pltpu.make_async_copy(made, table, small.at[2])
        copy.start()
        copy.wait()

        def step(i, carry):
            arrive(i + 1)
            for u in range(GROUP):
                turn(i + 1, u)
                local_row(table, staged, sources, total, i * GROUP + u, nnz)
            return carry

        lax.fori_loop(0, steps - 1, step, 0)
        for u in range(GROUP):
            local_row(table, staged, sources, total, (steps - 1) * GROUP + u, nnz)

    def in_hbm(array):
        return pltpu.with_memory_space_constraint(array, pltpu.HBM)

    return pl.pallas_call(
        kernel,
        out_shape=(
            shape(tiles.shape, tiles.dtype),
            shape((modes, width), jnp.float32),
            shape(table_shape, jnp.int32),
            shape((2 * rows + 8,), jnp.int32),
        ),
        in_specs=[SMEM, HBM, HBM, HBM, VMEM],
        out_specs=(VMEM, VMEM, SMEM, SMEM),
        scratch_shapes=[
            pltpu.VMEM((modes, width + tile), field.dtype),
            pltpu.VMEM(tiles.shape, tiles.dtype),
            pltpu.VMEM(tile_cols.shape, jnp.int32),
            pltpu.VMEM(table_shape, jnp.int32),
            pltpu.SMEM(send_rows.shape, jnp.int32),
            pltpu.SMEM((rows,), jnp.int32),
            pltpu.SemaphoreType.DMA((chunks,)),
            pltpu.SemaphoreType.DMA((3,)),
        ],
        compiler_params=params(16),
        cost_estimate=pl.CostEstimate(flops=2 * tiles.size * modes, bytes_accessed=2 * tiles.size, transcendentals=0),
        name="stage_and_sum",
    )(place, in_hbm(send_rows), in_hbm(tile_cols), in_hbm(tiles), field)


def local_sums(level, table, tiles, fields, rows, nnz):
    modes, tile = fields[0].shape[0], tiles.shape[1]
    width = rows * tile

    def kernel(table, tiles, *rest):
        *fields, total, sources = rest
        fill_sources(fields, sources)

        def step(i, carry):
            for u in range(GROUP):
                local_row(table, tiles, sources, total, i * GROUP + u, nnz)
            return carry

        lax.fori_loop(0, rows // GROUP, step, 0)

    return pl.pallas_call(
        kernel,
        out_shape=shape((modes, width), jnp.float32),
        in_specs=[SMEM] + [VMEM] * (1 + len(fields)),
        out_specs=VMEM,
        scratch_shapes=[pltpu.VMEM((modes, width + tile), fields[0].dtype)],
        compiler_params=params(8),
        cost_estimate=pl.CostEstimate(flops=tiles.size * modes // 8, bytes_accessed=0, transcendentals=0),
        name=f"local_sums_{level}",
    )(table, tiles, *fields)


def fill_ghosts(core, near, far, ghosts):
    width = near.shape[1]
    ghosts[:, columns(1 - core, width)] = near[...]
    ghosts[:, columns(core, width)] = far[...]
    ghosts[:, 2 * width :] = jnp.zeros((near.shape[0], ghosts.shape[1] - 2 * width), ghosts.dtype)


def ghost_rows(table, order, tiles, ghosts, partial, first, nnz):
    tile = tiles.shape[1]
    rows = [first + u if order is None else order[first + u] for u in range(GROUP)]
    most = table[3 * nnz, rows[0]]
    for row in rows[1:]:
        most = jnp.maximum(most, table[3 * nnz, row])
    usual = 3
    for u, row in enumerate(rows):
        positions = range(nnz - 2 * usual, nnz)
        partial[:, u * tile : (u + 1) * tile] = summed(table, tiles, ghosts, row, 1, positions, nnz)

    @pl.when(most > usual)
    def _():
        for u, row in enumerate(rows):
            here = slice(u * tile, (u + 1) * tile)
            partial[:, here] = partial[:, here] + summed(table, tiles, ghosts, row, 1, range(nnz - 2 * usual), nnz)

    return rows


def level_rows(level, bounds, rows, total, partial, field, previous, store):
    lower, upper = bounds
    modes, tile = field.shape[0], partial.shape[1] // GROUP
    center = (upper[0] + lower[0]) * 0.5
    factor = 1.0 / jnp.full((modes, tile), (upper[0] - lower[0]) * 0.5, jnp.float32)
    for u, row in enumerate(rows):
        here = columns(row, tile)
        value = total[:, here] + partial[:, u * tile : (u + 1) * tile]
        value = (value - center * field[:, here].astype(jnp.float32)) * factor
        if level == 2:
            value = 2.0 * value - previous[:, here].astype(jnp.float32)
        store(u, row, value.astype(field.dtype))


def next_lists(level, nnz, place, table, order, bounds, tiles, total, near, far, field, previous):
    tile = tiles.shape[1]

    def kernel(place, table, order, lower, upper, tiles, total, near, far, field, *rest):
        if level == 2:
            previous, *rest = rest
        else:
            previous = None
        new_far, new_near, ghosts, partial = rest
        fill_ghosts(place[1], near, far, ghosts)
        for out, first in ((new_far, 0), (new_near, GROUP)):
            rows = ghost_rows(table, order, tiles, ghosts, partial, first, nnz)

            def store(u, row, value, out=out):
                out[:, u * tile : (u + 1) * tile] = value

            level_rows(level, (lower, upper), rows, total, partial, field, previous, store)

    operands = [place, table, order, *bounds, tiles, total, near, far, field] + [previous] * (level == 2)
    return pl.pallas_call(
        kernel,
        out_shape=(shape(far.shape, far.dtype),) * 2,
        in_specs=[SMEM] * 5 + [VMEM] * (len(operands) - 5),
        out_specs=(VMEM,) * 2,
        scratch_shapes=[
            pltpu.VMEM((far.shape[0], 2 * far.shape[1] + tile), far.dtype),
            pltpu.VMEM((far.shape[0], GROUP * tile), jnp.float32),
        ],
        compiler_params=params(8),
        name=f"next_lists_{level}",
    )(*operands)


def next_level(level, nnz, place, table, order, bounds, tiles, total, near, far, field, previous, new_far, new_near):
    modes, width = field.shape
    tile = tiles.shape[1]

    def kernel(place, table, order, lower, upper, tiles, total, near, far, field, new_far, new_near, *rest):
        if level == 2:
            previous, *rest = rest
        else:
            previous = None
        out, ghosts, partial = rest
        fill_ghosts(place[1], near, far, ghosts)
        for held, first in ((new_far, 0), (new_near, GROUP)):
            for u in range(GROUP):
                out[:, columns(order[first + u], tile)] = held[:, u * tile : (u + 1) * tile]

        def store(u, row, value):
            out[:, columns(row, tile)] = value

        def step(i, carry):
            rows = ghost_rows(table, order, tiles, ghosts, partial, i * GROUP, nnz)
            level_rows(level, (lower, upper), rows, total, partial, field, previous, store)
            return carry

        lax.fori_loop(2, order[2 * width // tile], step, 0)

    operands = [place, table, order, *bounds, tiles, total, near, far, field, new_far, new_near]
    operands += [previous] * (level == 2)
    return pl.pallas_call(
        kernel,
        out_shape=shape(field.shape, field.dtype),
        in_specs=[SMEM] * 5 + [VMEM] * (len(operands) - 5),
        out_specs=VMEM,
        scratch_shapes=[
            pltpu.VMEM((modes, 2 * far.shape[1] + tile), far.dtype),
            pltpu.VMEM((modes, GROUP * tile), jnp.float32),
        ],
        compiler_params=params(8),
        cost_estimate=pl.CostEstimate(flops=tiles.size * modes, bytes_accessed=2 * tiles.size, transcendentals=0),
        name=f"next_level_{level}",
    )(*operands)


def last_level(nnz, place, table, send_rows, bounds, tiles, total, near, far, field, previous):
    modes, width = field.shape
    tile = tiles.shape[1]
    split = FIRST_PART * tile

    def kernel(place, table, send, lower, upper, tiles, total, near, far, field, previous, *rest):
        first, second, new_far, new_near, whole, ghosts, partial = rest
        core = place[1]
        fill_ghosts(core, near, far, ghosts)

        def store(u, row, value):
            whole[:, columns(row, tile)] = value

        def step(i, carry):
            rows = ghost_rows(table, None, tiles, ghosts, partial, i * GROUP, nnz)
            level_rows(2, (lower, upper), rows, total, partial, field, previous, store)
            return carry

        lax.fori_loop(0, width // tile // GROUP, step, 0)
        first[...] = whole[:, :split]
        second[...] = whole[:, split:]
        for slot in range(far.shape[1] // tile):
            here = slice(slot * tile, (slot + 1) * tile)
            new_far[:, here] = whole[:, columns(send[core, slot], tile)]
            new_near[:, here] = whole[:, columns(send[1 - core, slot], tile)]

    part = shape(far.shape, far.dtype)
    parts = [shape((modes, part_width), field.dtype) for part_width in (split, width - split)]
    return pl.pallas_call(
        kernel,
        out_shape=(*parts, part, part),
        in_specs=[SMEM] * 5 + [VMEM] * 6,
        out_specs=(VMEM,) * 4,
        scratch_shapes=[
            pltpu.VMEM((modes, width), field.dtype),
            pltpu.VMEM((modes, 2 * far.shape[1] + tile), far.dtype),
            pltpu.VMEM((modes, GROUP * tile), jnp.float32),
        ],
        compiler_params=params(8),
        name="last_level",
    )(place, table, send_rows, *bounds, tiles, total, near, far, field, previous)


def image_rows(nnz, place, table, tiles, total, near, far):
    modes, width = total.shape
    tile = tiles.shape[1]

    def kernel(place, table, tiles, total, near, far, out, ghosts, partial):
        fill_ghosts(place[1], near, far, ghosts)

        def step(i, carry):
            rows = ghost_rows(table, None, tiles, ghosts, partial, i * GROUP, nnz)
            for u, row in enumerate(rows):
                here = columns(row, tile)
                out[:, here] = (total[:, here] + partial[:, u * tile : (u + 1) * tile]).astype(out.dtype)
            return carry

        lax.fori_loop(0, width // tile // GROUP, step, 0)

    return pl.pallas_call(
        kernel,
        out_shape=shape((modes, width), near.dtype),
        in_specs=[SMEM] * 2 + [VMEM] * 4,
        out_specs=VMEM,
        scratch_shapes=[
            pltpu.VMEM((modes, 2 * near.shape[1] + tile), near.dtype),
            pltpu.VMEM((modes, GROUP * tile), jnp.float32),
        ],
        compiler_params=params(8),
        cost_estimate=pl.CostEstimate(flops=IMAGE_COST, bytes_accessed=0, transcendentals=0),
        name="image_rows",
    )(place, table, tiles, total, near, far)


def partial_sums(place, own, partner, image):
    modes, width = image.shape
    product = shape((modes, 2 * modes), jnp.float32)

    def kernel(place, own_first, own_second, first, second, image, keep, send, both, left):
        mode, core = place[0], place[1]
        split = own_first.shape[1]
        for out, row, parts in (
            (both, mode, (own_first, own_second)),
            (both, 1 - mode, (first, second)),
            (left, core, (own_first, own_second)),
        ):
            out[columns(row, modes), :split] = parts[0][...]
            out[columns(row, modes), split:] = parts[1][...]
        left[columns(1 - core, modes), :] = image[...]
        sums = lax.dot_general(left[...], both[...], NT, preferred_element_type=jnp.float32)
        keep[...] = sums[:modes]
        send[...] = sums[modes:]

    return pl.pallas_call(
        kernel,
        out_shape=(product, product, shape((2 * modes, width), image.dtype)),
        in_specs=[SMEM] + [VMEM] * 5,
        out_specs=(VMEM,) * 3,
        scratch_shapes=[pltpu.VMEM((2 * modes, width), image.dtype)],
        compiler_params=params(12),
        name="partial_sums",
    )(place, *own, *partner, image)


def sum_over_chips(value):
    for axis in (X, Y, Z):
        others = [flipped(value, axis, bits) for bits in (1, 3, 2)]
        value = (value + others[0]) + (others[1] + others[2])
    return value


def spread(block, lane):
    return jnp.broadcast_to(block[:, lane : lane + 1], block.shape)


def eliminated(blocks):
    rows, size = blocks[0].shape
    sub = lax.broadcasted_iota(jnp.int32, (rows, size), 0)
    lane = lax.broadcasted_iota(jnp.int32, (rows, size), 1)
    blocks = list(blocks)
    for b in range(len(blocks)):
        first = rows * b
        row = [jnp.broadcast_to(blocks[b][s : s + 1, :], (rows, size)) for s in range(rows)]
        d = {(t, s): spread(row[t], first + s) for t in range(rows) for s in range(t + 1)}
        unit = [row[s] + (lane == first + s).astype(jnp.float32) for s in range(rows)]
        ratio, reciprocal = {}, []
        for s in range(rows):
            reciprocal.append(1.0 / d[s, s])
            for t in range(s + 1, rows):
                ratio[t, s] = d[t, s] * reciprocal[s]
            for t in range(s + 1, rows):
                for q in range(s + 1, t + 1):
                    d[t, q] = d[t, q] - ratio[t, s] * d[q, s]
                unit[t] = unit[t] - ratio[t, s] * unit[s]
        solved = [None] * rows
        for s in reversed(range(rows)):
            value = unit[s] * reciprocal[s]
            for t in reversed(range(s + 1, rows)):
                value = value - ratio[t, s] * solved[t]
            solved[s] = value
        for k in range(b + 1, len(blocks)):
            value = blocks[k]
            for s in reversed(range(rows)):
                value = value - spread(blocks[k], first + s) * solved[s]
            blocks[k] = value
        value = blocks[b]
        for s in range(rows):
            value = jnp.where(sub == s, unit[s] - (lane == first + s).astype(jnp.float32), value)
        blocks[b] = value
    return blocks


def factor_and_project(place, quarters, both, dof_total):
    modes, width = both.shape[0] // 2, both.shape[1]
    size = 2 * modes

    def kernel(place, own, other_core, other_mode, last, both, basis, ritz, sums, inverse):
        mode, core = place[0], place[1]
        for part, c, m in (
            (own, core, mode),
            (other_core, 1 - core, mode),
            (other_mode, core, 1 - mode),
            (last, 1 - core, 1 - mode),
        ):
            sums[columns(2 * c + m, modes), :] = part[...] / dof_total
        blocks = eliminated([sums[i : i + 8, :] for i in range(0, size, 8)])
        matrix = jnp.concatenate(blocks, axis=0)
        sub = lax.broadcasted_iota(jnp.int32, (size, size), 0)
        lane = lax.broadcasted_iota(jnp.int32, (size, size), 1)
        pivots = jnp.sum(jnp.where(sub == lane, matrix, 0.0), axis=1, keepdims=True)
        lower = jnp.where(lane < sub, matrix, jnp.where(lane == sub, 1.0, 0.0)) * lax.rsqrt(pivots)
        inverse[...] = lower
        left = inverse[columns(mode, modes), :].astype(both.dtype)
        basis[...] = jnp.dot(left, both[...], preferred_element_type=jnp.float32).astype(basis.dtype)
        half = lax.dot_general(
            lower, sums[size:, :], NT, precision=lax.Precision.HIGHEST, preferred_element_type=jnp.float32
        )
        ritz[...] = lax.dot_general(
            half, lower, NT, precision=lax.Precision.HIGHEST, preferred_element_type=jnp.float32
        )

    return pl.pallas_call(
        kernel,
        out_shape=(shape((modes, width), both.dtype), shape((size, size), jnp.float32)),
        in_specs=[SMEM] + [VMEM] * 5,
        out_specs=(VMEM, VMEM),
        scratch_shapes=[pltpu.VMEM((2 * size, size), jnp.float32), pltpu.VMEM((size, size), jnp.float32)],
        compiler_params=params(12),
        name="factor_and_project",
    )(place, *quarters, both)


def shards(stiffness_tiles, tile_cols, send_rows, block, lower_bound, upper_bound):
    rows, nnz, tile, _ = stiffness_tiles.shape
    dof_total = block.shape[0] * lax.axis_size(DOF)
    place = jnp.stack([lax.axis_index(M), lax.axis_index(C)]).astype(jnp.int32)
    bounds = (lower_bound, upper_bound)

    level_0, far, near = pick_lists(place, send_rows, block.T, tile)
    far, near = swapped_between_chips(far), flipped(near, C, 1)
    tiles, total, table, order = stage_and_sum(
        place, send_rows, tile_cols.T, stiffness_tiles.reshape(rows * nnz, tile, tile), level_0
    )

    def exchange(near, far):
        return flipped(near, C, 1), swapped_between_chips(far)

    known = (nnz, place, table, order, bounds, tiles, total, near, far, level_0, None)
    far, near = next_lists(1, *known)
    level_1 = next_level(1, *known, far, near)
    near, far = exchange(near, far)
    total = local_sums(2, table, tiles, (level_1,), rows, nnz)

    *filtered, far, near = last_level(
        nnz, place, table, send_rows, bounds, tiles, total, near, far, level_1, level_0
    )
    near, far = exchange(near, far)
    partner = [flipped(part, M, 1) for part in filtered]
    total = local_sums(3, table, tiles, filtered, rows, nnz)
    image = image_rows(nnz, place, table, tiles, total, near, far)
    keep, send, both = partial_sums(place, filtered, partner, image)
    quarter = sum_over_chips(keep + flipped(send, C, 1))
    quarters = (quarter, flipped(quarter, C, 1), flipped(quarter, M, 1), flipped(quarter, (C, M), 3))
    basis, ritz = factor_and_project(place, quarters, both, dof_total)
    return (basis.T, ritz)


def solution(mesh):
    torus = Mesh(mesh.devices.reshape(4, 4, 4, 2, mesh.shape["mode"]), DOF + (M,))
    return jax.shard_map(
        shards,
        mesh=torus,
        in_specs=(P(DOF, None, None, None), P(DOF, None), P(DOF, None), P(DOF, M), P(), P()),
        out_specs=(P(DOF, M), P()),
        check_vma=False,
    )
```
